512 devices in a mesh: section: 16 (over z), chan: 32 (over y, x, core).
Axes of the slice: x: 4, y: 4, z: 16, core: 2. Of those that a mesh axis runs over, the one named last changes fastest.
Arguments:
- inputs: bfloat16 [4, 512, 256], P(None, 'chan'), may hold values from -6 to 6
- front: bfloat16 [16, 512, 256], P('section', 'chan'), may hold values from -6 to 6
- back: bfloat16 [16, 512, 256], P('section', 'chan'), may hold values from -6 to 6
- saved: bfloat16 [16, 4, 512, 256], P('section', None, 'chan'), may hold values from -6 to 6
- weights: bfloat16 [16, 512, 27, 512], P('section', 'chan'), may hold values from -0.1875 to 0.1875
- cotangent: bfloat16 [4, 512, 256], P(None, 'chan'), may hold values from -6 to 6
Outputs:
- acts: bfloat16 [16, 4, 512, 256], P('section', None, 'chan')
- grads: bfloat16 [16, 4, 512, 256], P('section', None, 'chan')
- weight_grads: float32 [16, 512, 27, 512], P('section', 'chan')
The draws below stay inside these ranges and needn't reach their ends.
All inputs are finite; a program needn't handle non-finite values.
Results may differ from the reference program's by a relative error of at most 0.035.
Values may be sent and summed in bfloat16 or wider, within the bound.
No kernel may reach another device: no remote copies, remote signals or barrier semaphores. Data moves between devices by JAX's collectives and lax.ppermute only.
A program may use at most 128 MiB of HBM per device.

```python
import jax
import jax.numpy as jnp
from jax import lax

C = 512
SX = 4
SY = 8
SZ = 8
ROUNDS = 4
SECTIONS = 16
CELLS = 256


def raised(array, stream_key, source, target, parts, factor):
    owner, partner = [(jnp.arange(array.shape[dim]) // (array.shape[dim] // parts)).reshape([-1 if axis == dim else 1 for axis in range(array.ndim)]) for dim in (source, target)]
    chosen = jax.random.permutation(stream_key, parts)[partner]
    strong = (owner == chosen) | (owner == (partner + parts // 2) % parts)
    return jnp.where(strong, factor * array, array)


def level_of(stream_key, extent, cuts, least, high):
    gain, own = 1.0, jax.random.fold_in(stream_key, 6)
    for dim, blocks in cuts:
        steps = jnp.exp(jax.random.uniform(jax.random.fold_in(own, dim), (blocks,), jnp.float32, least / len(cuts), high / len(cuts)))
        gain = gain * jnp.repeat(steps, extent[dim] // blocks).reshape([-1 if axis == dim else 1 for axis in range(len(extent))])
    return gain


def bell_draw(key, dims, scale, most, shards=(), held_as=jnp.bfloat16):
    loudness = level_of(key, dims, shards, -0.22, 0.18) if shards else 1.0
    result = jax.random.normal(key, dims, jnp.float32) * scale * loudness
    return jnp.minimum(jnp.maximum(result, -most), most).astype(held_as)


def noise_with(rng, dims, scale, limit, cuts, heavy, held_as=jnp.bfloat16):
    array = scale * jax.random.normal(rng, dims, jnp.float32)
    if cuts:
        array = array * level_of(rng, dims, cuts, -0.22, 0.18)
    return jnp.clip(raised(array, jax.random.fold_in(rng, 3), *heavy), -limit, limit).astype(held_as)


def setup_inputs(seed: int = 0) -> dict:
    arg_keys = jax.random.split(jax.random.key(seed), 7)
    return {
        "inputs": bell_draw(arg_keys[0], (ROUNDS, C, CELLS), 1.0, 6.0, ((1, 32),)),
        "front": bell_draw(arg_keys[1], (SECTIONS, C, CELLS), 1.0, 6.0, ((0, 16), (1, 32))),
        "back": bell_draw(arg_keys[2], (SECTIONS, C, CELLS), 1.0, 6.0, ((0, 16), (1, 32))),
        "saved": bell_draw(arg_keys[3], (SECTIONS, ROUNDS, C, CELLS), 1.0, 6.0, ((0, 16), (2, 32))),
        "weights": noise_with(arg_keys[4], (SECTIONS, C, 27, C), (8 * C) ** -0.5, 0.1875, ((0, 16), (1, 32)), (1, 3, 32, 2.75)),
        "cotangent": bell_draw(arg_keys[5], (ROUNDS, C, CELLS), 1.0, 6.0, ((1, 32),)),
    }


TAP_OFFSETS = [(i - 1, j - 1, l - 1) for i in range(3) for j in range(3) for l in range(3)]


def shifted_view(values, offset):
    cell_count = SX * SY * SZ
    margin = SY * SZ + SZ + 1
    lead = values.ndim - 1
    padded = jnp.pad(values, [(0, 0)] * lead + [(margin, margin)])
    delta = offset[0] * SY * SZ + offset[1] * SZ + offset[2]
    moved = padded[..., margin + delta:margin + delta + cell_count]
    index = jnp.arange(cell_count, dtype=jnp.int32)
    first_pos = index // (SY * SZ) + offset[0]
    second_pos = (index // SZ) % SY + offset[1]
    third_pos = index % SZ + offset[2]
    inside = (first_pos >= 0) & (first_pos < SX) & (second_pos >= 0) & (second_pos < SY) & (third_pos >= 0) & (third_pos < SZ)
    return jnp.where(inside, moved, jnp.zeros_like(moved))


def tap_sum(taps):
    accum = shifted_view(taps[..., 0, :], TAP_OFFSETS[0])
    for index in range(1, 27):
        accum = accum + shifted_view(taps[..., index, :], TAP_OFFSETS[index])
    return accum


def tap_spread(values):
    return jnp.stack([shifted_view(values, (-o[0], -o[1], -o[2])) for o in TAP_OFFSETS], axis=-2)


def silu_slope(pre):
    logistic = jax.nn.sigmoid(pre)
    return logistic * (1.0 + pre * (1.0 - logistic))


def conv_pre(filters, layer_in):
    taps = jnp.dot(filters.reshape(C * 27, C), layer_in, preferred_element_type=jnp.float32)
    return tap_sum(taps.reshape(C, 27, SX * SY * SZ))


def forward_layer(pair):
    filters, layer_in = pair
    return jax.nn.silu(conv_pre(filters, layer_in)).astype(jnp.bfloat16)


def backward_layer(triple):
    filters, stored, grad_out = triple
    cell_count = SX * SY * SZ
    pre = conv_pre(filters, stored)
    dpre = (grad_out.astype(jnp.float32) * silu_slope(pre)).astype(jnp.bfloat16)
    spread = tap_spread(dpre).reshape(C * 27, cell_count)
    grad_in = lax.dot_general(filters.reshape(C * 27, C), spread, (((0,), (0,)), ((), ())), preferred_element_type=jnp.float32).astype(jnp.bfloat16)
    filter_grad = jnp.dot(spread, stored.T, preferred_element_type=jnp.float32)
    return grad_in, filter_grad


def reference(inputs, front, back, saved, weights, cotangent):
    acts_list = []
    grads_list = []
    weight_total = jnp.zeros((SECTIONS, C * 27, C), jnp.float32)
    previous_out = None
    previous_grad = None
    for round_index in range(ROUNDS):
        if round_index == 0:
            incoming = front.at[0].set(inputs[0])
            arriving = back.at[SECTIONS - 1].set(cotangent[0])
        else:
            incoming = jnp.concatenate([inputs[round_index][None], previous_out[:-1]], axis=0)
            arriving = jnp.concatenate([previous_grad[1:], cotangent[round_index][None]], axis=0)
        layer_out = lax.map(forward_layer, (weights, incoming))
        grad_in, filter_grad = lax.map(backward_layer, (weights, saved[:, round_index], arriving))
        acts_list.append(layer_out)
        grads_list.append(grad_in)
        weight_total = weight_total + filter_grad
        previous_out = layer_out
        previous_grad = grad_in
    acts = jnp.stack(acts_list, axis=1)
    grads = jnp.stack(grads_list, axis=1)
    return acts, grads, weight_total.reshape(SECTIONS, C, 27, C)
```

```python
import jax
import jax.numpy as jnp
from jax import lax
from jax.sharding import PartitionSpec as P

SX = 4
SY = 8
SZ = 8


TAP_OFFSETS = [(i - 1, j - 1, l - 1) for i in range(3) for j in range(3) for l in range(3)]


def from_behind(value, axis, steps):
    count = lax.axis_size(axis)
    first, last = (max(0, -steps), min(count, count - steps))
    return lax.ppermute(value, axis, [(source, source + steps) for source in range(first, last)])


def shifted_view(values, offset):
    cell_count = SX * SY * SZ
    margin = SY * SZ + SZ + 1
    lead = values.ndim - 1
    padded = jnp.pad(values, [(0, 0)] * lead + [(margin, margin)])
    delta = offset[0] * SY * SZ + offset[1] * SZ + offset[2]
    moved = padded[..., margin + delta : margin + delta + cell_count]
    index = jnp.arange(cell_count, dtype=jnp.int32)
    first_pos = index // (SY * SZ) + offset[0]
    second_pos = index // SZ % SY + offset[1]
    third_pos = index % SZ + offset[2]
    inside = (
        (first_pos >= 0)
        & (first_pos < SX)
        & (second_pos >= 0)
        & (second_pos < SY)
        & (third_pos >= 0)
        & (third_pos < SZ)
    )
    return jnp.where(inside, moved, jnp.zeros_like(moved))


def tap_sum(taps):
    accum = shifted_view(taps[..., 0, :], TAP_OFFSETS[0])
    for index in range(1, 27):
        accum = accum + shifted_view(taps[..., index, :], TAP_OFFSETS[index])
    return accum


def tap_spread(values):
    return jnp.stack([shifted_view(values, (-o[0], -o[1], -o[2])) for o in TAP_OFFSETS], axis=-2)


def silu_slope(pre):
    logistic = jax.nn.sigmoid(pre)
    return logistic * (1.0 + pre * (1.0 - logistic))


def gathered(block, axis):
    count = lax.axis_size(axis)
    copies = jnp.broadcast_to(block[None], (count,) + block.shape)
    return lax.all_to_all(copies, axis, 0, 0).reshape(count * block.shape[0], block.shape[1])


def scattered_sum(parts, axis):
    count = lax.axis_size(axis)
    blocks = lax.all_to_all(parts.reshape(count, parts.shape[0] // count, parts.shape[1]), axis, 0, 0)
    return jnp.sum(blocks.astype(jnp.float32), axis=0).astype(parts.dtype)


def body(inputs, front, back, saved, weights, cotangent):
    section_count = lax.axis_size("section")
    section_index = lax.axis_index("section")
    first_section = section_index == 0
    last_section = section_index == section_count - 1
    round_count, own_filters, cell_count = inputs.shape
    channels = weights.shape[3]
    weight_rows = weights.reshape(own_filters * 27, channels)
    acts_list = []
    grads_list = []
    filter_grad = jnp.zeros((own_filters * 27, channels), jnp.float32)
    forward_recv = front[0]
    backward_recv = back[0]
    for round_index in range(round_count):
        layer_in = jnp.where(first_section, inputs[round_index], forward_recv)
        taps = jnp.dot(
            weight_rows,
            gathered(layer_in, "chan"),
            preferred_element_type=jnp.float32,
        )
        pre = tap_sum(taps.reshape(own_filters, 27, cell_count))
        layer_out = jax.nn.silu(pre).astype(jnp.bfloat16)
        acts_list.append(layer_out)
        if round_index + 1 < round_count:
            forward_recv = from_behind(layer_out, "section", 1)
        whole_in = gathered(saved[0, round_index], "chan")
        back_taps = jnp.dot(weight_rows, whole_in, preferred_element_type=jnp.float32)
        pre_back = tap_sum(back_taps.reshape(own_filters, 27, cell_count))
        grad_out = jnp.where(last_section, cotangent[round_index], backward_recv)
        dpre = (grad_out.astype(jnp.float32) * silu_slope(pre_back)).astype(jnp.bfloat16)
        spread = tap_spread(dpre).reshape(own_filters * 27, cell_count)
        grad_in = scattered_sum(
            lax.dot_general(
                weight_rows, spread, (((0,), (0,)), ((), ())), preferred_element_type=jnp.float32
            ).astype(jnp.bfloat16),
            "chan",
        )
        filter_grad = filter_grad + lax.dot_general(
            spread, whole_in, (((1,), (1,)), ((), ())), preferred_element_type=jnp.float32
        )
        grads_list.append(grad_in)
        if round_index + 1 < round_count:
            backward_recv = from_behind(grad_in, "section", -1)
    acts = jnp.stack(acts_list, axis=0)[None]
    grads = jnp.stack(grads_list, axis=0)[None]
    return (acts, grads, filter_grad.reshape(1, own_filters, 27, channels))


def solution(mesh):
    return jax.shard_map(
        body,
        mesh=mesh,
        in_specs=(
            P(None, "chan", None),
            P("section", "chan", None),
            P("section", "chan", None),
            P("section", None, "chan", None),
            P("section", "chan", None, None),
            P(None, "chan", None),
        ),
        out_specs=(
            P("section", None, "chan", None),
            P("section", None, "chan", None),
            P("section", "chan", None, None),
        ),
        check_vma=False,
    )
```

```python
import jax
import jax.numpy as jnp
from jax import lax
from jax.experimental import pallas as pl
from jax.experimental.pallas import tpu as pltpu
from jax.sharding import Mesh, PartitionSpec as P


SX, SY, SZ = 4, 8, 8
CELLS = SX * SY * SZ
TAPS = 27
OWN = 16
PAIR = 32
ROUNDS = 4
CHANNELS = 512
ROWS = TAPS * OWN
STEPS = (SY * SZ, SZ, 1)
EXTENT = (SX, SY, SZ)
VMEM_LIMIT = 48 * 1024 * 1024


def coordinates(rows):
    cell = lax.broadcasted_iota(jnp.int32, (rows, CELLS), 1)
    return (cell >> 6, (cell >> 3) & 7, cell & 7)


def moved(value, where, axis, step):
    if step == 0:
        return value
    rolled = pltpu.roll(value, (-step * STEPS[axis]) % CELLS, 1)
    place = where[axis]
    inside = place < EXTENT[axis] - 1 if step > 0 else place > 0
    return jnp.where(inside, rolled, 0.0)


def tap_total(taps, base, where):
    total = None
    for i in range(3):
        plane = None
        for j in range(3):
            line = None
            for l in range(3):
                start = base + OWN * (9 * i + 3 * j + l)
                term = moved(taps[start : start + OWN, :], where, 2, l - 1)
                line = term if line is None else line + term
            line = moved(line, where, 1, j - 1)
            plane = line if plane is None else plane + line
        plane = moved(plane, where, 0, i - 1)
        total = plane if total is None else total + plane
    return total


def spread_into(spread, base, value, where):
    for i in range(3):
        plane = moved(value, where, 0, 1 - i)
        for j in range(3):
            line = moved(plane, where, 1, 1 - j)
            for l in range(3):
                start = base + OWN * (9 * i + 3 * j + l)
                spread[start : start + OWN, :] = moved(line, where, 2, 1 - l).astype(jnp.bfloat16)


def slope_kernel(filters, stored, slope, taps):
    where = coordinates(OWN)
    for r in range(stored.shape[1]):
        whole = stored[:, r].reshape(CHANNELS, CELLS)
        taps[...] = jnp.dot(filters[...], whole, preferred_element_type=jnp.float32)
        for c in range(2):
            pre = tap_total(taps, ROWS * c, where)
            logistic = 1.0 / (1.0 + jnp.exp(-pre))
            slope[r, OWN * c : OWN * (c + 1), :] = logistic * (1.0 + pre * (1.0 - logistic))


def finish_kernel(flags, arrived, filters, out, taps):
    @pl.when(flags[0] == 0)
    def _():
        where = coordinates(OWN)
        whole = arrived[...].reshape(CHANNELS, CELLS)
        taps[...] = jnp.dot(filters[...], whole, preferred_element_type=jnp.float32)
        for c in range(2):
            pre = tap_total(taps, ROWS * c, where)
            out[OWN * c : OWN * (c + 1), :] = (pre / (1.0 + jnp.exp(-pre))).astype(jnp.bfloat16)

    @pl.when(flags[0] != 0)
    def _():
        total = arrived[0].astype(jnp.float32)
        for p in range(1, arrived.shape[0]):
            total = total + arrived[p].astype(jnp.float32)
        out[...] = total.astype(jnp.bfloat16)


def start_kernel(edge_slot, flags, received, outside, slope, filters, sent, dpre, spread):
    take = flags[edge_slot] != 0
    value = jnp.where(take, outside[...].astype(jnp.float32), received[...].astype(jnp.float32))

    @pl.when(flags[0] == 0)
    def _():
        copy = value.astype(jnp.bfloat16)
        dpre[...] = copy
        for p in range(sent.shape[0]):
            sent[p] = copy

    @pl.when(flags[0] != 0)
    def _():
        where = coordinates(OWN)
        rounded = (value * slope[...]).astype(jnp.bfloat16)
        dpre[...] = rounded
        wide = rounded.astype(jnp.float32)
        for c in range(2):
            spread_into(spread, ROWS * c, wide[OWN * c : OWN * (c + 1), :], where)
        part = lax.dot_general(
            filters[...], spread[...], (((0,), (0,)), ((), ())), preferred_element_type=jnp.float32
        )
        sent[...] = part.astype(jnp.bfloat16).reshape(sent.shape)


def filter_kernel(dpre, first, later, out, spread):
    where = coordinates(OWN)
    for r in range(ROUNDS):
        spread_into(spread, 0, dpre[r].astype(jnp.float32), where)
        stored = first[:, 0] if r == 0 else later[:, r - 1]
        term = lax.dot_general(
            spread[...],
            stored.reshape(CHANNELS, CELLS),
            (((1,), (1,)), ((), ())),
            preferred_element_type=jnp.float32,
        )
        if r == 0:
            out[...] = term
        else:
            out[...] += term


def local_call(kernel, outs, kinds, scratch):
    spaces = {"s": pltpu.SMEM, "v": pltpu.VMEM}
    specs = [pl.BlockSpec(memory_space=spaces[kind]) for kind in kinds]
    result = jax.tree.map(lambda _: pl.BlockSpec(memory_space=pltpu.VMEM), outs)
    return pl.pallas_call(
        kernel,
        out_shape=outs,
        in_specs=specs,
        out_specs=result,
        scratch_shapes=scratch,
        compiler_params=pltpu.CompilerParams(vmem_limit_bytes=VMEM_LIMIT),
    )


def shape(dims, dtype=jnp.bfloat16):
    return jax.ShapeDtypeStruct(dims, dtype)


def gathered(block, axes, count):
    copies = jnp.broadcast_to(block[None], (count,) + block.shape)
    return lax.all_to_all(copies, axes, 0, 0)


def body(sections, inputs, front, back, saved, weights, cotangent):
    chips = CHANNELS // PAIR
    section = lax.axis_index("section")
    core = lax.axis_index("core")
    forward = core == 0
    at_edge = jnp.where(forward, section == 0, section == sections - 1)
    flags = jnp.stack([core, at_edge.astype(jnp.int32), jnp.int32(1)]).astype(jnp.int32)
    hop_pairs = []
    for s in range(sections):
        for p in range(chips):
            here = (s * chips + p) * 2
            if s + 1 < sections:
                hop_pairs.append((here, here + 2 * chips))
            if s > 0:
                hop_pairs.append((here + 1, here + 1 - 2 * chips))

    everyone = ("chip", "core")
    stored_first = gathered(saved[0, :1], everyone, 2 * chips)
    stored_later = gathered(saved[0, 1:], everyone, 2 * chips)

    filters = lax.all_gather(
        jnp.transpose(weights[0], (1, 0, 2)).reshape(ROWS, CHANNELS), "core", axis=0, tiled=True
    )
    ends = jnp.concatenate(
        [
            jnp.where(section == 0, inputs[:1], front),
            inputs[1:],
            jnp.where(section == sections - 1, cotangent[:1], back),
            cotangent[1:],
        ]
    )
    ends = lax.all_gather(ends, "core", axis=1, tiled=True)
    outside = jnp.where(forward, ends[:ROUNDS], ends[ROUNDS:])

    taps_scratch = pltpu.VMEM((2 * ROWS, CELLS), jnp.float32)
    spread_scratch = pltpu.VMEM((2 * ROWS, CELLS), jnp.bfloat16)
    slope_of = lambda stored, n: local_call(
        slope_kernel, shape((n, PAIR, CELLS), jnp.float32), "vv", [taps_scratch]
    )(filters, stored)
    slopes = [slope_of(stored_first, 1)[0]]

    outs, dpres = [], []
    received = outside[0]
    for r in range(ROUNDS):
        edge_slot = 2 if r == 0 else 1
        sent, dpre = local_call(
            lambda *refs: start_kernel(edge_slot, *refs),
            (shape((chips, PAIR, CELLS)), shape((PAIR, CELLS))),
            "svvvv",
            [spread_scratch],
        )(flags, received, outside[r], slopes[r], filters)
        dpres.append(dpre)
        arrived = lax.all_to_all(sent, "chip", 0, 0)
        if r == 0:
            rest = slope_of(stored_later, ROUNDS - 1)
            slopes.extend(rest[n] for n in range(ROUNDS - 1))
        out = local_call(finish_kernel, shape((PAIR, CELLS)), "svv", [taps_scratch])(flags, arrived, filters)
        outs.append(out)
        if r + 1 < ROUNDS:
            received = lax.ppermute(out, ("section", "chip", "core"), hop_pairs)

    both = jnp.stack(dpres)
    for_other = lax.ppermute(both[:, :OWN], "core", [(1, 0)])
    dpre_own = jnp.where(forward, for_other, both[:, OWN:])
    filter_grad = local_call(
        filter_kernel, shape((ROWS, CHANNELS), jnp.float32), "vvv", [pltpu.VMEM((ROWS, CELLS), jnp.bfloat16)]
    )(dpre_own, stored_first, stored_later)

    chain = jnp.stack(outs)
    swapped = lax.ppermute(jnp.where(forward, chain[:, OWN:], chain[:, :OWN]), "core", [(0, 1), (1, 0)])
    acts = jnp.where(forward, chain[:, :OWN], swapped)
    grads = jnp.where(forward, swapped, chain[:, OWN:])
    filter_grad = jnp.transpose(filter_grad.reshape(TAPS, OWN, CHANNELS), (1, 0, 2))
    return acts[None], grads[None], filter_grad[None]


def solution(mesh):
    sections = mesh.shape["section"]
    fine = Mesh(mesh.devices.reshape(sections, -1, 2), ("section", "chip", "core"))
    chan = ("chip", "core")
    return jax.shard_map(
        lambda *arrays: body(sections, *arrays),
        mesh=fine,
        in_specs=(
            P(None, chan, None),
            P("section", chan, None),
            P("section", chan, None),
            P("section", None, chan, None),
            P("section", chan, None, None),
            P(None, chan, None),
        ),
        out_specs=(
            P("section", None, chan, None),
            P("section", None, chan, None),
            P("section", chan, None, None),
        ),
        check_vma=False,
    )
```

```python
import jax
import jax.numpy as jnp
from jax import lax
from jax.experimental import pallas as pl
from jax.experimental.pallas import tpu as pltpu
from jax.sharding import Mesh, PartitionSpec as P


SX, SY, SZ = 4, 8, 8
CELLS = SX * SY * SZ
TAPS = 27
OWN = 16
PAIR = 32
ROUNDS = 4
CHANNELS = 512
ROWS = TAPS * OWN
STEPS = (SY * SZ, SZ, 1)
EXTENT = (SX, SY, SZ)
VMEM_LIMIT = 48 * 1024 * 1024


def coordinates(rows):
    cell = lax.broadcasted_iota(jnp.int32, (rows, CELLS), 1)
    return (cell >> 6, (cell >> 3) & 7, cell & 7)


def moved(value, where, axis, step):
    if step == 0:
        return value
    rolled = pltpu.roll(value, (-step * STEPS[axis]) % CELLS, 1)
    place = where[axis]
    inside = place < EXTENT[axis] - 1 if step > 0 else place > 0
    return jnp.where(inside, rolled, 0.0)


def tap_total(taps, base, where):
    total = None
    for i in range(3):
        plane = None
        for j in range(3):
            line = None
            for l in range(3):
                start = base + OWN * (9 * i + 3 * j + l)
                term = moved(taps[start : start + OWN, :], where, 2, l - 1)
                line = term if line is None else line + term
            line = moved(line, where, 1, j - 1)
            plane = line if plane is None else plane + line
        plane = moved(plane, where, 0, i - 1)
        total = plane if total is None else total + plane
    return total


def spread_into(spread, base, value, where):
    for i in range(3):
        plane = moved(value, where, 0, 1 - i)
        for j in range(3):
            line = moved(plane, where, 1, 1 - j)
            for l in range(3):
                start = base + OWN * (9 * i + 3 * j + l)
                spread[start : start + OWN, :] = moved(line, where, 2, 1 - l).astype(jnp.bfloat16)


def slope_of(filters, whole, taps, where):
    taps[...] = jnp.dot(filters[...], whole.reshape(CHANNELS, CELLS), preferred_element_type=jnp.float32)
    parts = []
    for c in range(2):
        pre = tap_total(taps, ROWS * c, where)
        logistic = 1.0 / (1.0 + jnp.exp(-pre))
        parts.append(logistic * (1.0 + pre * (1.0 - logistic)))
    return parts


def slope_kernel(filters, near, far, second, third, fourth, taps):
    where = coordinates(OWN)
    for stored, r, slope in ((near, 1, second), (far, 0, third), (far, 1, fourth)):
        parts = slope_of(filters, stored[:, r], taps, where)
        for c in range(2):
            slope[OWN * c : OWN * (c + 1), :] = parts[c]


def finish_kernel(flags, arrived, filters, out, taps):
    @pl.when(flags[0] == 0)
    def _():
        where = coordinates(OWN)
        whole = arrived[...].reshape(CHANNELS, CELLS)
        taps[...] = jnp.dot(filters[...], whole, preferred_element_type=jnp.float32)
        for c in range(2):
            pre = tap_total(taps, ROWS * c, where)
            out[OWN * c : OWN * (c + 1), :] = (pre / (1.0 + jnp.exp(-pre))).astype(jnp.bfloat16)

    @pl.when(flags[0] != 0)
    def _():
        total = arrived[0].astype(jnp.float32)
        for p in range(1, arrived.shape[0]):
            total = total + arrived[p].astype(jnp.float32)
        out[...] = total.astype(jnp.bfloat16)


def send_copies(value, sent):
    for p in range(sent.shape[0]):
        sent[p] = value


def send_parts(rounded, filters, sent, spread, where):
    for c in range(2):
        wide = rounded[OWN * c : OWN * (c + 1), :].astype(jnp.float32)
        spread_into(spread, ROWS * c, wide, where)
    part = lax.dot_general(
        filters[...], spread[...], (((0,), (0,)), ((), ())), preferred_element_type=jnp.float32
    )
    sent[...] = part.astype(jnp.bfloat16).reshape(sent.shape)


def first_kernel(flags, outside, near, filters, sent, dpre, spread, taps):
    @pl.when(flags[0] == 0)
    def _():
        dpre[...] = outside[...]
        send_copies(outside[...], sent)

    @pl.when(flags[0] != 0)
    def _():
        where = coordinates(OWN)
        parts = slope_of(filters, near[:, 0], taps, where)
        for c in range(2):
            rows = slice(OWN * c, OWN * (c + 1))
            dpre[rows, :] = (outside[rows, :].astype(jnp.float32) * parts[c]).astype(jnp.bfloat16)
        send_parts(dpre, filters, sent, spread, where)


def start_kernel(flags, received, outside, slope, filters, sent, dpre, spread):
    take = flags[1] != 0
    value = jnp.where(take, outside[...].astype(jnp.float32), received[...].astype(jnp.float32))

    @pl.when(flags[0] == 0)
    def _():
        copy = value.astype(jnp.bfloat16)
        dpre[...] = copy
        send_copies(copy, sent)

    @pl.when(flags[0] != 0)
    def _():
        dpre[...] = (value * slope[...]).astype(jnp.bfloat16)
        send_parts(dpre, filters, sent, spread, coordinates(OWN))


def filter_kernel(flags, dpre, near, far, out, spread):
    where = coordinates(OWN)
    near_base = 2 * (1 - flags[0])
    far_base = 2 * flags[0]
    for n, (stored, r, base) in enumerate(((near, 0, near_base), (near, 1, near_base), (far, 0, far_base), (far, 1, far_base))):
        spread_into(spread, 0, dpre[base + r].astype(jnp.float32), where)
        term = lax.dot_general(
            spread[...],
            stored[:, r].reshape(CHANNELS, CELLS),
            (((1,), (1,)), ((), ())),
            preferred_element_type=jnp.float32,
        )
        if n == 0:
            out[...] = term
        else:
            out[...] += term


def local_call(kernel, outs, kinds, scratch):
    spaces = {"s": pltpu.SMEM, "v": pltpu.VMEM}
    specs = [pl.BlockSpec(memory_space=spaces[kind]) for kind in kinds]
    result = jax.tree.map(lambda _: pl.BlockSpec(memory_space=pltpu.VMEM), outs)
    return pl.pallas_call(
        kernel,
        out_shape=outs,
        in_specs=specs,
        out_specs=result,
        scratch_shapes=scratch,
        compiler_params=pltpu.CompilerParams(vmem_limit_bytes=VMEM_LIMIT),
    )


def shape(dims, dtype=jnp.bfloat16):
    return jax.ShapeDtypeStruct(dims, dtype)


def body(sections, inputs, front, back, saved, weights, cotangent):
    chips = CHANNELS // PAIR
    section = lax.axis_index("section")
    core = lax.axis_index("core")
    forward = core == 0
    at_edge = jnp.where(forward, section == 0, section == sections - 1)
    flags = jnp.stack([core, at_edge.astype(jnp.int32)]).astype(jnp.int32)
    hop_pairs = []
    for s in range(sections):
        for p in range(chips):
            here = (s * chips + p) * 2
            if s + 1 < sections:
                hop_pairs.append((here, here + 2 * chips))
            if s > 0:
                hop_pairs.append((here + 1, here + 1 - 2 * chips))

    stored = lax.all_gather(saved[0], "core", axis=1, tiled=True)
    stored = jnp.where(forward, stored[2:], stored[:2])
    near = lax.all_to_all(jnp.broadcast_to(stored[None], (chips,) + stored.shape), "chip", 0, 0)
    far = lax.ppermute(near, "core", [(0, 1), (1, 0)])

    filters = lax.all_gather(
        jnp.transpose(weights[0], (1, 0, 2)).reshape(ROWS, CHANNELS), "core", axis=0, tiled=True
    )
    ends = jnp.concatenate(
        [
            jnp.where(section == 0, inputs[:1], front),
            inputs[1:],
            jnp.where(section == sections - 1, cotangent[:1], back),
            cotangent[1:],
        ]
    )
    ends = lax.all_gather(ends, "core", axis=1, tiled=True)
    outside = jnp.where(forward, ends[:ROUNDS], ends[ROUNDS:])

    taps_scratch = pltpu.VMEM((2 * ROWS, CELLS), jnp.float32)
    spread_scratch = pltpu.VMEM((2 * ROWS, CELLS), jnp.bfloat16)
    to_send = (shape((chips, PAIR, CELLS)), shape((PAIR, CELLS)))

    outs, dpres = [], []
    sent, dpre = local_call(first_kernel, to_send, "svvv", [spread_scratch, taps_scratch])(
        flags, outside[0], near, filters
    )
    for r in range(ROUNDS):
        dpres.append(dpre)
        arrived = lax.all_to_all(sent, "chip", 0, 0)
        if r == 0:
            slopes = local_call(
                slope_kernel, (shape((PAIR, CELLS), jnp.float32),) * 3, "vvv", [taps_scratch]
            )(filters, near, far)
        if r + 1 == ROUNDS:
            both = jnp.stack(dpres)
            for_other = lax.ppermute(both[:, :OWN], "core", [(1, 0)])
            dpre_own = jnp.where(forward, for_other, both[:, OWN:])
            filter_grad = local_call(
                filter_kernel,
                shape((ROWS, CHANNELS), jnp.float32),
                "svvv",
                [pltpu.VMEM((ROWS, CELLS), jnp.bfloat16)],
            )(flags, dpre_own, near, far)
            arrived, filter_grad = lax.optimization_barrier((arrived, filter_grad))
        out = local_call(finish_kernel, shape((PAIR, CELLS)), "svv", [taps_scratch])(flags, arrived, filters)
        outs.append(out)
        if r + 1 < ROUNDS:
            received = lax.ppermute(out, ("section", "chip", "core"), hop_pairs)
            sent, dpre = local_call(start_kernel, to_send, "svvvv", [spread_scratch])(
                flags, received, outside[r + 1], slopes[r], filters
            )

    chain = jnp.stack(outs)
    swapped = lax.ppermute(jnp.where(forward, chain[:, OWN:], chain[:, :OWN]), "core", [(0, 1), (1, 0)])
    acts = jnp.where(forward, chain[:, :OWN], swapped)
    grads = jnp.where(forward, swapped, chain[:, OWN:])
    filter_grad = jnp.transpose(filter_grad.reshape(TAPS, OWN, CHANNELS), (1, 0, 2))
    return acts[None], grads[None], filter_grad[None]


def solution(mesh):
    sections = mesh.shape["section"]
    fine = Mesh(mesh.devices.reshape(sections, -1, 2), ("section", "chip", "core"))
    chan = ("chip", "core")
    return jax.shard_map(
        lambda *arrays: body(sections, *arrays),
        mesh=fine,
        in_specs=(
            P(None, chan, None),
            P("section", chan, None),
            P("section", chan, None),
            P("section", None, chan, None),
            P("section", chan, None, None),
            P(None, chan, None),
        ),
        out_specs=(
            P("section", None, chan, None),
            P("section", None, chan, None),
            P("section", chan, None, None),
        ),
        check_vma=False,
    )
```

```python
import functools

import jax
import jax.numpy as jnp
from jax import lax
from jax.experimental import pallas as pl
from jax.experimental.pallas import tpu as pltpu
from jax.sharding import Mesh, PartitionSpec as P


SX, SY, SZ = 4, 8, 8
CELLS = SX * SY * SZ
TAPS = 27
OWN = 16
PAIR = 32
ROUNDS = 4
CHANNELS = 512
ROWS = TAPS * OWN
STEPS = (SY * SZ, SZ, 1)
EXTENT = (SX, SY, SZ)
VMEM_LIMIT = 16 * 1024 * 1024
LIGHT = pl.CostEstimate(flops=1, transcendentals=0, bytes_accessed=1)


def coordinates(rows):
    cell = lax.broadcasted_iota(jnp.int32, (rows, CELLS), 1)
    return (cell >> 6, (cell >> 3) & 7, cell & 7)


def moved(value, where, axis, step):
    if step == 0:
        return value
    rolled = pltpu.roll(value, (-step * STEPS[axis]) % CELLS, 1)
    place = where[axis]
    inside = place < EXTENT[axis] - 1 if step > 0 else place > 0
    return jnp.where(inside, rolled, 0.0)


def tap_total(taps, base, where):
    total = None
    for i in range(3):
        plane = None
        for j in range(3):
            line = None
            for l in range(3):
                start = base + OWN * (9 * i + 3 * j + l)
                term = moved(taps[start : start + OWN, :], where, 2, l - 1)
                line = term if line is None else line + term
            line = moved(line, where, 1, j - 1)
            plane = line if plane is None else plane + line
        plane = moved(plane, where, 0, i - 1)
        total = plane if total is None else total + plane
    return total


def spread_into(spread, base, value, where):
    for i in range(3):
        plane = moved(value, where, 0, 1 - i)
        for j in range(3):
            line = moved(plane, where, 1, 1 - j)
            for l in range(3):
                start = base + OWN * (9 * i + 3 * j + l)
                spread[start : start + OWN, :] = moved(line, where, 2, 1 - l).astype(jnp.bfloat16)


def slope_into(slope, filters, whole, taps, where):
    taps[...] = jnp.dot(filters[...], whole.reshape(CHANNELS, CELLS), preferred_element_type=jnp.float32)
    for c in range(2):
        pre = tap_total(taps, ROWS * c, where)
        logistic = 1.0 / (1.0 + jnp.exp(-pre))
        slope[OWN * c : OWN * (c + 1), :] = logistic * (1.0 + pre * (1.0 - logistic))


def silu_into(out, filters, whole, taps, where):
    taps[...] = jnp.dot(filters[...], whole.reshape(CHANNELS, CELLS), preferred_element_type=jnp.float32)
    for c in range(2):
        pre = tap_total(taps, ROWS * c, where)
        out[OWN * c : OWN * (c + 1), :] = (pre / (1.0 + jnp.exp(-pre))).astype(jnp.bfloat16)


def late_round(tails, r, whole):
    if r < 3:
        return tails[2 - r, :, 0:2]
    whole[:, 0] = tails[0, :, 2]
    whole[:, 1] = tails[1, :, 2]
    return whole[...]


def first_kernel(flags, near, filters, act, slope, taps):
    where = coordinates(OWN)

    @pl.when(flags[0] == 0)
    def _():
        silu_into(act, filters, near[:, 0:2], taps, where)
        slope[...] = jnp.zeros_like(slope)

    @pl.when(flags[0] != 0)
    def _():
        act[...] = jnp.zeros_like(act)
        slope_into(slope, filters, near[:, 0:2], taps, where)


def slope_kernel(flags, filters, tails, second, third, fourth, taps, whole):
    @pl.when(flags[0] == 0)
    def _():
        for slope in (second, third, fourth):
            slope[...] = jnp.zeros_like(slope)

    @pl.when(flags[0] != 0)
    def _():
        where = coordinates(OWN)
        for r, slope in enumerate((second, third, fourth)):
            slope_into(slope, filters, late_round(tails, r + 1, whole), taps, where)


def sum_into(out, arrived):
    total = arrived[0].astype(jnp.float32)
    for p in range(1, arrived.shape[0]):
        total = total + arrived[p].astype(jnp.float32)
    out[...] = total.astype(jnp.bfloat16)


def finish_kernel(flags, arrived, filters, out, taps):
    @pl.when(flags[0] == 0)
    def _():
        silu_into(out, filters, arrived[...], taps, coordinates(OWN))

    @pl.when(flags[0] != 0)
    def _():
        sum_into(out, arrived)


def sum_kernel(flags, arrived, out):
    @pl.when(flags[0] == 0)
    def _():
        out[...] = jnp.zeros_like(out)

    @pl.when(flags[0] != 0)
    def _():
        sum_into(out, arrived)


def pack_kernel(flags, arrived, filters, *refs):
    (*outs, grad), dpres, (act, parcel, taps) = refs[:4], refs[4:8], refs[8:]

    @pl.when(flags[0] == 0)
    def _():
        silu_into(act, filters, arrived[...], taps, coordinates(OWN))
        for r, pair in enumerate((*outs, act)):
            parcel[r] = pair[OWN:, :]
        for r in range(ROUNDS - 1):
            parcel[ROUNDS + r] = jnp.zeros((OWN, CELLS), jnp.bfloat16)

    @pl.when(flags[0] != 0)
    def _():
        act[...] = jnp.zeros_like(act)
        for r, pair in enumerate((*dpres, *outs[1:], grad)):
            parcel[r] = pair[:OWN, :]


def last_kernel(flags, arrived, parcels, second, third, fourth, grads):
    for r, pair in enumerate((second, third, fourth)):
        odd = pair[OWN:, :].astype(jnp.float32)
        even = parcels[1, ROUNDS + r].astype(jnp.float32)
        grads[r] = jnp.where(flags[0] == 0, even, odd).astype(jnp.bfloat16)
    total = arrived[1].astype(jnp.float32)
    for d in range(3, arrived.shape[0], 2):
        total = total + arrived[d].astype(jnp.float32)
    grads[ROUNDS - 1] = total.astype(jnp.bfloat16)


def start_kernel(edge_slot, last, flags, received, outside, slope, filters, sent, dpre, spread):
    take = flags[edge_slot] != 0
    value = jnp.where(take, outside[...].astype(jnp.float32), received[...].astype(jnp.float32))

    @pl.when(flags[0] == 0)
    def _():
        copy = value.astype(jnp.bfloat16)
        dpre[...] = copy
        if last:
            sent[...] = jnp.zeros_like(sent)
        else:
            for p in range(sent.shape[0]):
                sent[p] = copy

    @pl.when(flags[0] != 0)
    def _():
        where = coordinates(OWN)
        rounded = (value * slope[...]).astype(jnp.bfloat16)
        dpre[...] = rounded
        wide = rounded.astype(jnp.float32)
        for c in range(2):
            spread_into(spread, ROWS * c, wide[OWN * c : OWN * (c + 1), :], where)
        part = lax.dot_general(
            filters[...], spread[...], (((0,), (0,)), ((), ())), preferred_element_type=jnp.float32
        )
        sent[...] = part.astype(jnp.bfloat16).reshape(sent.shape)


def filter_kernel(flags, heads, tails, parcels, *refs):
    acts_pair, dpres, (out, acts, spread, whole) = refs[:4], refs[4:8], refs[8:]
    where = coordinates(OWN)
    even_core = flags[0] == 0
    for r in range(ROUNDS):
        own = acts_pair[r][:OWN, :].astype(jnp.float32)
        acts[r] = jnp.where(even_core, own, parcels[0, r].astype(jnp.float32)).astype(jnp.bfloat16)
        own = dpres[r][OWN:, :].astype(jnp.float32)
        spread_into(spread, 0, jnp.where(even_core, parcels[1, r].astype(jnp.float32), own), where)
        term = lax.dot_general(
            spread[...],
            (late_round(tails, r, whole) if r else heads[1]).reshape(CHANNELS, CELLS),
            (((1,), (1,)), ((), ())),
            preferred_element_type=jnp.float32,
        )
        if r == 0:
            out[...] = term
        else:
            out[...] += term


def local_call(kernel, outs, kinds, scratch, cost=None):
    spaces = {"s": pltpu.SMEM, "v": pltpu.VMEM}
    specs = [pl.BlockSpec(memory_space=spaces[kind]) for kind in kinds]
    result = jax.tree.map(lambda _: pl.BlockSpec(memory_space=pltpu.VMEM), outs)
    return pl.pallas_call(
        kernel,
        out_shape=outs,
        in_specs=specs,
        out_specs=result,
        scratch_shapes=scratch,
        compiler_params=pltpu.CompilerParams(vmem_limit_bytes=VMEM_LIMIT),
        cost_estimate=cost,
    )


def shape(dims, dtype=jnp.bfloat16):
    return jax.ShapeDtypeStruct(dims, dtype)


def body(sections, inputs, front, back, saved, weights, cotangent):
    chips = CHANNELS // PAIR
    section = lax.axis_index("section")
    core = lax.axis_index("core")
    forward = core == 0
    at_edge = jnp.where(forward, section == 0, section == sections - 1)
    from_outside = jnp.where(forward, section == 0, True)
    flags = jnp.stack([core, from_outside.astype(jnp.int32), at_edge.astype(jnp.int32)]).astype(jnp.int32)
    ahead, behind = [], []
    for s in range(sections - 1):
        for p in range(chips):
            here = (s * chips + p) * 2
            ahead.append((here, here + 2 * chips))
            behind.append((here + 1 + 2 * chips, here + 1))
    hops = [ahead, ahead + behind, ahead + behind, behind]

    known = lax.all_gather(
        jnp.concatenate([jnp.where(section == 0, inputs[:1], front), saved[0]]), "core", axis=1, tiled=True
    )
    block = jnp.where(
        forward,
        jnp.concatenate([known[0], known[3], known[4, :OWN]]),
        jnp.concatenate([known[1], known[2], known[4, OWN:]]),
    ).reshape(5, OWN, CELLS)
    near = lax.all_to_all(jnp.broadcast_to(block[None], (chips,) + block.shape), "chip", 0, 0)

    filters = lax.all_gather(
        jnp.transpose(weights[0], (1, 0, 2)).reshape(ROWS, CHANNELS), "core", axis=0, tiled=True
    )
    ends = jnp.concatenate(
        [inputs[1:], jnp.where(section == sections - 1, cotangent[:1], back), cotangent[1:]]
    )
    ends = lax.all_gather(ends, "core", axis=1, tiled=True)
    outside = jnp.where(forward, jnp.concatenate([ends[:3], ends[2:3]]), ends[3:])

    taps_scratch = pltpu.VMEM((2 * ROWS, CELLS), jnp.float32)
    spread_scratch = pltpu.VMEM((2 * ROWS, CELLS), jnp.bfloat16)
    whole_scratch = pltpu.VMEM((chips, 2, OWN, CELLS), jnp.bfloat16)
    mine, slope_shape = shape((PAIR, CELLS)), shape((PAIR, CELLS), jnp.float32)

    act, slope = local_call(first_kernel, (mine, slope_shape), "svv", [taps_scratch])(flags, near, filters)
    slopes = [slope]
    outs, dpres = [act], []
    for step in range(ROUNDS):
        last = step + 1 == ROUNDS
        received = lax.ppermute(outs[step], ("section", "chip", "core"), hops[step])
        sent_shape = shape((2 * chips, OWN, CELLS) if last else (chips, PAIR, CELLS))
        sent, dpre = local_call(
            functools.partial(start_kernel, 1 if step == 0 else 2, last),
            (sent_shape, mine),
            "svvvv",
            [spread_scratch],
        )(flags, received, outside[step], slopes[step], filters)
        dpres.append(dpre)
        if last:
            break
        if step == 0:
            sent, near = lax.optimization_barrier((sent, near))
        arrived = lax.all_to_all(sent, "chip", 0, 0)
        if step == 0:
            tails = lax.all_gather(near[:, 2:], "core", axis=0)
            heads = lax.all_gather(near[:, :2], "core", axis=0)
            rest = local_call(slope_kernel, (slope_shape,) * 3, "svv", [taps_scratch, whole_scratch], LIGHT)(
                flags, filters, tails
            )
            arrived, heads, *rest = lax.optimization_barrier((arrived, heads, *rest))
            slopes.extend(rest)
        if step + 2 < ROUNDS:
            out = local_call(finish_kernel, mine, "svv", [taps_scratch])(flags, arrived, filters)
        else:
            out = local_call(sum_kernel, mine, "sv", [])(flags, arrived)
        outs.append(out)

    sent, arrived = lax.optimization_barrier((sent, arrived))
    partials = lax.all_to_all(sent, ("chip", "core"), 0, 0)
    act, parcel = local_call(
        pack_kernel, (mine, shape((2 * ROUNDS - 1, OWN, CELLS))), "svv" + "v" * 8, [taps_scratch], LIGHT
    )(flags, arrived, filters, *outs, *dpres)
    parcels = lax.all_gather(parcel, "core", axis=0)
    filter_grad, acts = local_call(
        filter_kernel,
        (shape((ROWS, CHANNELS), jnp.float32), shape((ROUNDS, OWN, CELLS))),
        "svvv" + "v" * 8,
        [pltpu.VMEM((ROWS, CELLS), jnp.bfloat16), whole_scratch],
        LIGHT,
    )(flags, heads, tails, parcels, *outs[:3], act, *dpres)
    partials, filter_grad = lax.optimization_barrier((partials, filter_grad))
    grads = local_call(last_kernel, shape((ROUNDS, OWN, CELLS)), "svvvvv", [])(
        flags, partials, parcels, *outs[1:]
    )
    filter_grad = jnp.transpose(filter_grad.reshape(TAPS, OWN, CHANNELS), (1, 0, 2))
    return acts[None], grads[None], filter_grad[None]


def solution(mesh):
    sections = mesh.shape["section"]
    fine = Mesh(mesh.devices.reshape(sections, -1, 2), ("section", "chip", "core"))
    chan = ("chip", "core")
    return jax.shard_map(
        lambda *arrays: body(sections, *arrays),
        mesh=fine,
        in_specs=(
            P(None, chan, None),
            P("section", chan, None),
            P("section", chan, None),
            P("section", None, chan, None),
            P("section", chan, None, None),
            P(None, chan, None),
        ),
        out_specs=(
            P("section", None, chan, None),
            P("section", None, chan, None),
            P("section", chan, None, None),
        ),
        check_vma=False,
    )
```

```python
import functools

import jax
import jax.numpy as jnp
from jax import lax
from jax.experimental import pallas as pl
from jax.experimental.pallas import tpu as pltpu
from jax.sharding import Mesh, PartitionSpec as P


SX, SY, SZ = 4, 8, 8
CELLS = SX * SY * SZ
TAPS = 27
OWN = 16
PAIR = 32
ROUNDS = 4
CHANNELS = 512
ROWS = TAPS * OWN
STEPS = (SY * SZ, SZ, 1)
EXTENT = (SX, SY, SZ)
VMEM_LIMIT = 16 * 1024 * 1024
LIGHT = pl.CostEstimate(flops=1, transcendentals=0, bytes_accessed=1)


def coordinates(rows):
    cell = lax.broadcasted_iota(jnp.int32, (rows, CELLS), 1)
    return (cell >> 6, (cell >> 3) & 7, cell & 7)


def moved(value, where, axis, step):
    if step == 0:
        return value
    rolled = pltpu.roll(value, (-step * STEPS[axis]) % CELLS, 1)
    place = where[axis]
    inside = place < EXTENT[axis] - 1 if step > 0 else place > 0
    return jnp.where(inside, rolled, 0.0)


def tap_total(taps, base, where):
    total = None
    for i in range(3):
        plane = None
        for j in range(3):
            line = None
            for l in range(3):
                start = base + OWN * (9 * i + 3 * j + l)
                term = moved(taps[start : start + OWN, :], where, 2, l - 1)
                line = term if line is None else line + term
            line = moved(line, where, 1, j - 1)
            plane = line if plane is None else plane + line
        plane = moved(plane, where, 0, i - 1)
        total = plane if total is None else total + plane
    return total


def spread_into(spread, base, value, where):
    for i in range(3):
        plane = moved(value, where, 0, 1 - i)
        for j in range(3):
            line = moved(plane, where, 1, 1 - j)
            for l in range(3):
                start = base + OWN * (9 * i + 3 * j + l)
                spread[start : start + OWN, :] = moved(line, where, 2, 1 - l).astype(jnp.bfloat16)


def slope_into(slope, filters, whole, taps, where):
    taps[...] = jnp.dot(filters[...], whole.reshape(CHANNELS, CELLS), preferred_element_type=jnp.float32)
    for c in range(2):
        pre = tap_total(taps, ROWS * c, where)
        logistic = 1.0 / (1.0 + jnp.exp(-pre))
        slope[OWN * c : OWN * (c + 1), :] = logistic * (1.0 + pre * (1.0 - logistic))


def silu_into(out, filters, whole, taps, where):
    taps[...] = jnp.dot(filters[...], whole.reshape(CHANNELS, CELLS), preferred_element_type=jnp.float32)
    for c in range(2):
        pre = tap_total(taps, ROWS * c, where)
        out[OWN * c : OWN * (c + 1), :] = (pre / (1.0 + jnp.exp(-pre))).astype(jnp.bfloat16)


def joined(even, odd, whole):
    whole[:, 0] = even[:, 4]
    whole[:, 1] = odd[:, 4]
    return whole[...]


def first_kernel(flags, near, filters, act, first, second, taps):
    where = coordinates(OWN)

    @pl.when(flags[0] == 0)
    def _():
        silu_into(act, filters, near[:, 0:2], taps, where)
        for slope in (first, second):
            slope[...] = jnp.zeros_like(slope)

    @pl.when(flags[0] != 0)
    def _():
        act[...] = jnp.zeros_like(act)
        slope_into(first, filters, near[:, 0:2], taps, where)
        slope_into(second, filters, near[:, 2:4], taps, where)


def slope_kernel(flags, filters, near, far, third, fourth, taps, whole):
    @pl.when(flags[0] == 0)
    def _():
        for slope in (third, fourth):
            slope[...] = jnp.zeros_like(slope)

    @pl.when(flags[0] != 0)
    def _():
        where = coordinates(OWN)
        slope_into(third, filters, far[:, 2:4], taps, where)
        slope_into(fourth, filters, joined(far, near, whole), taps, where)


def sum_into(out, arrived):
    total = arrived[0].astype(jnp.float32)
    for p in range(1, arrived.shape[0]):
        total = total + arrived[p].astype(jnp.float32)
    out[...] = total.astype(jnp.bfloat16)


def finish_kernel(flags, arrived, filters, out, taps):
    @pl.when(flags[0] == 0)
    def _():
        silu_into(out, filters, arrived[...], taps, coordinates(OWN))

    @pl.when(flags[0] != 0)
    def _():
        sum_into(out, arrived)


def pack_kernel(flags, *refs):
    outs, dpres, parcel = refs[:4], refs[4:8], refs[8]

    @pl.when(flags[0] == 0)
    def _():
        for r, pair in enumerate(outs):
            parcel[r] = pair[OWN:, :]
        for r in range(ROUNDS - 1):
            parcel[ROUNDS + r] = jnp.zeros((OWN, CELLS), jnp.bfloat16)

    @pl.when(flags[0] != 0)
    def _():
        for r, pair in enumerate((*dpres, *outs[1:])):
            parcel[r] = pair[:OWN, :]


def last_kernel(flags, arrived, parcels, second, third, fourth, grads):
    for r, pair in enumerate((second, third, fourth)):
        odd = pair[OWN:, :].astype(jnp.float32)
        even = parcels[1, ROUNDS + r].astype(jnp.float32)
        grads[r] = jnp.where(flags[0] == 0, even, odd).astype(jnp.bfloat16)
    total = arrived[1].astype(jnp.float32)
    for d in range(3, arrived.shape[0], 2):
        total = total + arrived[d].astype(jnp.float32)
    grads[ROUNDS - 1] = total.astype(jnp.bfloat16)


def start_kernel(edge_slot, last, flags, received, outside, slope, filters, sent, dpre, spread):
    take = flags[edge_slot] != 0
    value = jnp.where(take, outside[...].astype(jnp.float32), received[...].astype(jnp.float32))

    @pl.when(flags[0] == 0)
    def _():
        copy = value.astype(jnp.bfloat16)
        dpre[...] = copy
        if last:
            sent[...] = jnp.zeros_like(sent)
        else:
            for p in range(sent.shape[0]):
                sent[p] = copy

    @pl.when(flags[0] != 0)
    def _():
        where = coordinates(OWN)
        rounded = (value * slope[...]).astype(jnp.bfloat16)
        dpre[...] = rounded
        wide = rounded.astype(jnp.float32)
        for c in range(2):
            spread_into(spread, ROWS * c, wide[OWN * c : OWN * (c + 1), :], where)
        part = lax.dot_general(
            filters[...], spread[...], (((0,), (0,)), ((), ())), preferred_element_type=jnp.float32
        )
        sent[...] = part.astype(jnp.bfloat16).reshape(sent.shape)


def filter_kernel(flags, near, far, parcels, *refs):
    acts_pair, dpres, (out, acts, spread, whole) = refs[:4], refs[4:8], refs[8:]

    def total(even, odd, act_of, dpre_of):
        where = coordinates(OWN)
        stored = (
            lambda: odd[:, 0:2],
            lambda: odd[:, 2:4],
            lambda: even[:, 2:4],
            lambda: joined(even, odd, whole),
        )
        for r in range(ROUNDS):
            acts[r] = act_of(r)
            spread_into(spread, 0, dpre_of(r).astype(jnp.float32), where)
            term = lax.dot_general(
                spread[...],
                stored[r]().reshape(CHANNELS, CELLS),
                (((1,), (1,)), ((), ())),
                preferred_element_type=jnp.float32,
            )
            if r == 0:
                out[...] = term
            else:
                out[...] += term

    @pl.when(flags[0] == 0)
    def _():
        total(near, far, lambda r: acts_pair[r][:OWN, :], lambda r: parcels[1, r])

    @pl.when(flags[0] != 0)
    def _():
        total(far, near, lambda r: parcels[0, r], lambda r: dpres[r][OWN:, :])


def local_call(kernel, outs, kinds, scratch, cost=None):
    spaces = {"s": pltpu.SMEM, "v": pltpu.VMEM}
    specs = [pl.BlockSpec(memory_space=spaces[kind]) for kind in kinds]
    result = jax.tree.map(lambda _: pl.BlockSpec(memory_space=pltpu.VMEM), outs)
    return pl.pallas_call(
        kernel,
        out_shape=outs,
        in_specs=specs,
        out_specs=result,
        scratch_shapes=scratch,
        compiler_params=pltpu.CompilerParams(vmem_limit_bytes=VMEM_LIMIT),
        cost_estimate=cost,
    )


def shape(dims, dtype=jnp.bfloat16):
    return jax.ShapeDtypeStruct(dims, dtype)


def body(sections, inputs, front, back, saved, weights, cotangent):
    chips = CHANNELS // PAIR
    section = lax.axis_index("section")
    core = lax.axis_index("core")
    forward = core == 0
    at_edge = jnp.where(forward, section == 0, section == sections - 1)
    from_outside = jnp.where(forward, section == 0, True)
    flags = jnp.stack([core, from_outside.astype(jnp.int32), at_edge.astype(jnp.int32)]).astype(jnp.int32)
    ahead, behind = [], []
    for s in range(sections - 1):
        for p in range(chips):
            here = (s * chips + p) * 2
            ahead.append((here, here + 2 * chips))
            behind.append((here + 1 + 2 * chips, here + 1))
    hops = [ahead, ahead + behind, ahead + behind, behind]

    known = lax.all_gather(
        jnp.concatenate([jnp.where(section == 0, inputs[:1], front), saved[0]]), "core", axis=1, tiled=True
    )
    block = jnp.where(
        forward,
        jnp.concatenate([known[0], known[3], known[4, :OWN]]),
        jnp.concatenate([known[1], known[2], known[4, OWN:]]),
    ).reshape(5, OWN, CELLS)
    near = lax.all_to_all(jnp.broadcast_to(block[None], (chips,) + block.shape), "chip", 0, 0)

    filters = lax.all_gather(
        jnp.transpose(weights[0], (1, 0, 2)).reshape(ROWS, CHANNELS), "core", axis=0, tiled=True
    )
    ends = jnp.concatenate(
        [inputs[1:], jnp.where(section == sections - 1, cotangent[:1], back), cotangent[1:]]
    )
    ends = lax.all_gather(ends, "core", axis=1, tiled=True)
    outside = jnp.where(forward, jnp.concatenate([ends[:3], ends[2:3]]), ends[3:])

    taps_scratch = pltpu.VMEM((2 * ROWS, CELLS), jnp.float32)
    spread_scratch = pltpu.VMEM((2 * ROWS, CELLS), jnp.bfloat16)
    whole_scratch = pltpu.VMEM((chips, 2, OWN, CELLS), jnp.bfloat16)
    mine, slope_shape = shape((PAIR, CELLS)), shape((PAIR, CELLS), jnp.float32)

    act, *slopes = local_call(first_kernel, (mine, slope_shape, slope_shape), "svv", [taps_scratch])(
        flags, near, filters
    )
    after = lax.optimization_barrier
    outs, dpres = [act], []
    for step in range(ROUNDS):
        last = step + 1 == ROUNDS
        outs[step], near, filters = after((outs[step], near, filters))
        received = lax.ppermute(outs[step], ("section", "chip", "core"), hops[step])
        if step == 0:
            far = lax.ppermute(near, "core", [(0, 1), (1, 0)])
        elif step == 2:
            rest = local_call(slope_kernel, (slope_shape,) * 2, "svvv", [taps_scratch, whole_scratch], LIGHT)(
                flags, filters, near, far
            )
            received, *rest = after((received, *rest))
            slopes.extend(rest)
        sent_shape = shape((2 * chips, OWN, CELLS) if last else (chips, PAIR, CELLS))
        sent, dpre = local_call(
            functools.partial(start_kernel, 1 if step == 0 else 2, last),
            (sent_shape, mine),
            "svvvv",
            [spread_scratch],
        )(flags, received, outside[step], slopes[step], filters)
        dpres.append(dpre)
        if last:
            break
        arrived = lax.all_to_all(sent, "chip", 0, 0)
        outs.append(local_call(finish_kernel, mine, "svv", [taps_scratch])(flags, arrived, filters))

    sent, *dpres = after((sent, *dpres))
    partials = lax.all_to_all(sent, ("chip", "core"), 0, 0)
    parcel = local_call(pack_kernel, shape((2 * ROUNDS - 1, OWN, CELLS)), "s" + "v" * 8, [], LIGHT)(
        flags, *outs, *dpres
    )
    parcels = lax.all_gather(parcel, "core", axis=0)
    filter_grad, acts = local_call(
        filter_kernel,
        (shape((ROWS, CHANNELS), jnp.float32), shape((ROUNDS, OWN, CELLS))),
        "svvv" + "v" * 8,
        [pltpu.VMEM((ROWS, CELLS), jnp.bfloat16), whole_scratch],
        LIGHT,
    )(flags, near, far, parcels, *outs, *dpres)
    partials, filter_grad = lax.optimization_barrier((partials, filter_grad))
    grads = local_call(last_kernel, shape((ROUNDS, OWN, CELLS)), "svvvvv", [])(
        flags, partials, parcels, *outs[1:]
    )
    filter_grad = jnp.transpose(filter_grad.reshape(TAPS, OWN, CHANNELS), (1, 0, 2))
    return acts[None], grads[None], filter_grad[None]


def solution(mesh):
    sections = mesh.shape["section"]
    fine = Mesh(mesh.devices.reshape(sections, -1, 2), ("section", "chip", "core"))
    chan = ("chip", "core")
    return jax.shard_map(
        lambda *arrays: body(sections, *arrays),
        mesh=fine,
        in_specs=(
            P(None, chan, None),
            P("section", chan, None),
            P("section", chan, None),
            P("section", None, chan, None),
            P("section", chan, None, None),
            P(None, chan, None),
        ),
        out_specs=(
            P("section", None, chan, None),
            P("section", None, chan, None),
            P("section", chan, None, None),
        ),
        check_vma=False,
    )
```

```python
import functools

import jax
import jax.numpy as jnp
from jax import lax
from jax.experimental import pallas as pl
from jax.experimental.pallas import tpu as pltpu
from jax.sharding import Mesh, PartitionSpec as P


SX, SY, SZ = 4, 8, 8
CELLS = SX * SY * SZ
TAPS = 27
OWN = 16
PAIR = 32
ROUNDS = 4
CHANNELS = 512
ROWS = TAPS * OWN
STEPS = (SY * SZ, SZ, 1)
EXTENT = (SX, SY, SZ)
VMEM_LIMIT = 16 * 1024 * 1024
LIGHT = pl.CostEstimate(flops=1, transcendentals=0, bytes_accessed=1)


def coordinates(rows):
    cell = lax.broadcasted_iota(jnp.int32, (rows, CELLS), 1)
    return (cell >> 6, (cell >> 3) & 7, cell & 7)


def moved(value, where, axis, step):
    if step == 0:
        return value
    rolled = pltpu.roll(value, (-step * STEPS[axis]) % CELLS, 1)
    place = where[axis]
    inside = place < EXTENT[axis] - 1 if step > 0 else place > 0
    return jnp.where(inside, rolled, 0.0)


def tap_total(taps, base, where):
    total = None
    for i in range(3):
        plane = None
        for j in range(3):
            line = None
            for l in range(3):
                start = base + OWN * (9 * i + 3 * j + l)
                term = moved(taps[start : start + OWN, :], where, 2, l - 1)
                line = term if line is None else line + term
            line = moved(line, where, 1, j - 1)
            plane = line if plane is None else plane + line
        plane = moved(plane, where, 0, i - 1)
        total = plane if total is None else total + plane
    return total


def spread_into(spread, base, value, where):
    for i in range(3):
        plane = moved(value, where, 0, 1 - i)
        for j in range(3):
            line = moved(plane, where, 1, 1 - j)
            for l in range(3):
                start = base + OWN * (9 * i + 3 * j + l)
                spread[start : start + OWN, :] = moved(line, where, 2, 1 - l).astype(jnp.bfloat16)


def slope_into(slope, filters, whole, taps, where):
    taps[...] = jnp.dot(filters[...], whole.reshape(CHANNELS, CELLS), preferred_element_type=jnp.float32)
    for c in range(2):
        pre = tap_total(taps, ROWS * c, where)
        logistic = 1.0 / (1.0 + jnp.exp(-pre))
        slope[OWN * c : OWN * (c + 1), :] = logistic * (1.0 + pre * (1.0 - logistic))


def silu_into(out, filters, whole, taps, where):
    taps[...] = jnp.dot(filters[...], whole.reshape(CHANNELS, CELLS), preferred_element_type=jnp.float32)
    for c in range(2):
        pre = tap_total(taps, ROWS * c, where)
        out[OWN * c : OWN * (c + 1), :] = (pre / (1.0 + jnp.exp(-pre))).astype(jnp.bfloat16)


def joined(even, odd, whole):
    whole[:, 0] = even[:, 4]
    whole[:, 1] = odd[:, 4]
    return whole[...]


def first_kernel(near, filters, act, first, second, taps):
    where = coordinates(OWN)

    @pl.when(lax.axis_index("core") == 0)
    def _():
        silu_into(act, filters, near[:, 0:2], taps, where)
        for slope in (first, second):
            slope[...] = jnp.zeros_like(slope)

    @pl.when(lax.axis_index("core") != 0)
    def _():
        act[...] = jnp.zeros_like(act)
        slope_into(first, filters, near[:, 0:2], taps, where)
        slope_into(second, filters, near[:, 2:4], taps, where)


def slope_kernel(filters, near, far, third, fourth, taps, whole):
    @pl.when(lax.axis_index("core") == 0)
    def _():
        for slope in (third, fourth):
            slope[...] = jnp.zeros_like(slope)

    @pl.when(lax.axis_index("core") != 0)
    def _():
        where = coordinates(OWN)
        slope_into(third, filters, far[:, 2:4], taps, where)
        slope_into(fourth, filters, joined(far, near, whole), taps, where)


def sum_into(out, arrived):
    total = arrived[0].astype(jnp.float32)
    for p in range(1, arrived.shape[0]):
        total = total + arrived[p].astype(jnp.float32)
    out[...] = total.astype(jnp.bfloat16)


def finish_kernel(arrived, filters, out, taps):
    @pl.when(lax.axis_index("core") == 0)
    def _():
        silu_into(out, filters, arrived[...], taps, coordinates(OWN))

    @pl.when(lax.axis_index("core") != 0)
    def _():
        sum_into(out, arrived)


def pack_kernel(*refs):
    outs, dpres, parcel = refs[:4], refs[4:8], refs[8]

    @pl.when(lax.axis_index("core") == 0)
    def _():
        for r, pair in enumerate(outs):
            parcel[r] = pair[OWN:, :]
        for r in range(ROUNDS - 1):
            parcel[ROUNDS + r] = jnp.zeros((OWN, CELLS), jnp.bfloat16)

    @pl.when(lax.axis_index("core") != 0)
    def _():
        for r, pair in enumerate((*dpres, *outs[1:])):
            parcel[r] = pair[:OWN, :]


def last_kernel(arrived, parcels, second, third, fourth, grads):
    for r, pair in enumerate((second, third, fourth)):
        odd = pair[OWN:, :].astype(jnp.float32)
        even = parcels[1, ROUNDS + r].astype(jnp.float32)
        grads[r] = jnp.where(lax.axis_index("core") == 0, even, odd).astype(jnp.bfloat16)
    total = arrived[1].astype(jnp.float32)
    for d in range(3, arrived.shape[0], 2):
        total = total + arrived[d].astype(jnp.float32)
    grads[ROUNDS - 1] = total.astype(jnp.bfloat16)


def start_kernel(step, received, outside, slope, filters, sent, dpre, spread):
    last = step + 1 == ROUNDS
    section = lax.axis_index("section")
    edge = section == lax.axis_size("section") - 1
    backward_edge = True if step == 0 else edge
    take = jnp.where(lax.axis_index("core") == 0, section == 0, backward_edge)
    value = jnp.where(take, outside[...].astype(jnp.float32), received[...].astype(jnp.float32))

    @pl.when(lax.axis_index("core") == 0)
    def _():
        copy = value.astype(jnp.bfloat16)
        dpre[...] = copy
        if last:
            sent[...] = jnp.zeros_like(sent)
        else:
            for p in range(sent.shape[0]):
                sent[p] = copy

    @pl.when(lax.axis_index("core") != 0)
    def _():
        where = coordinates(OWN)
        rounded = (value * slope[...]).astype(jnp.bfloat16)
        dpre[...] = rounded
        wide = rounded.astype(jnp.float32)
        for c in range(2):
            spread_into(spread, ROWS * c, wide[OWN * c : OWN * (c + 1), :], where)
        part = lax.dot_general(
            filters[...], spread[...], (((0,), (0,)), ((), ())), preferred_element_type=jnp.float32
        )
        sent[...] = part.astype(jnp.bfloat16).reshape(sent.shape)


def filter_kernel(near, far, parcels, *refs):
    acts_pair, dpres, (out, acts, spread, whole) = refs[:4], refs[4:8], refs[8:]

    def total(even, odd, act_of, dpre_of):
        where = coordinates(OWN)
        stored = (
            lambda: odd[:, 0:2],
            lambda: odd[:, 2:4],
            lambda: even[:, 2:4],
            lambda: joined(even, odd, whole),
        )
        for r in range(ROUNDS):
            acts[r] = act_of(r)
            spread_into(spread, 0, dpre_of(r).astype(jnp.float32), where)
            term = lax.dot_general(
                spread[...],
                stored[r]().reshape(CHANNELS, CELLS),
                (((1,), (1,)), ((), ())),
                preferred_element_type=jnp.float32,
            )
            if r == 0:
                out[...] = term
            else:
                out[...] += term

    @pl.when(lax.axis_index("core") == 0)
    def _():
        total(near, far, lambda r: acts_pair[r][:OWN, :], lambda r: parcels[1, r])

    @pl.when(lax.axis_index("core") != 0)
    def _():
        total(far, near, lambda r: parcels[0, r], lambda r: dpres[r][OWN:, :])


def local_call(kernel, outs, count, scratch, cost=None):
    specs = [pl.BlockSpec(memory_space=pltpu.VMEM)] * count
    result = jax.tree.map(lambda _: pl.BlockSpec(memory_space=pltpu.VMEM), outs)
    return pl.pallas_call(
        kernel,
        out_shape=outs,
        in_specs=specs,
        out_specs=result,
        scratch_shapes=scratch,
        compiler_params=pltpu.CompilerParams(vmem_limit_bytes=VMEM_LIMIT),
        cost_estimate=cost,
    )


def shape(dims, dtype=jnp.bfloat16):
    return jax.ShapeDtypeStruct(dims, dtype)


def body(sections, inputs, front, back, saved, weights, cotangent):
    chips = CHANNELS // PAIR
    section = lax.axis_index("section")
    core = lax.axis_index("core")
    forward = core == 0
    ahead, behind = [], []
    for s in range(sections - 1):
        for p in range(chips):
            here = (s * chips + p) * 2
            ahead.append((here, here + 2 * chips))
            behind.append((here + 1 + 2 * chips, here + 1))
    hops = [ahead, ahead + behind, ahead + behind, behind]

    known = lax.all_gather(
        jnp.concatenate([jnp.where(section == 0, inputs[:1], front), saved[0]]), "core", axis=1, tiled=True
    )
    block = jnp.where(
        forward,
        jnp.concatenate([known[0], known[3], known[4, :OWN]]),
        jnp.concatenate([known[1], known[2], known[4, OWN:]]),
    ).reshape(5, OWN, CELLS)
    near = lax.all_to_all(jnp.broadcast_to(block[None], (chips,) + block.shape), "chip", 0, 0)

    filters = lax.all_gather(
        jnp.transpose(weights[0], (1, 0, 2)).reshape(ROWS, CHANNELS), "core", axis=0, tiled=True
    )
    ends = jnp.concatenate(
        [inputs[1:], jnp.where(section == sections - 1, cotangent[:1], back), cotangent[1:]]
    )
    ends = lax.all_gather(ends, "core", axis=1, tiled=True)
    outside = jnp.where(forward, jnp.concatenate([ends[:3], ends[2:3]]), ends[3:])

    taps_scratch = pltpu.VMEM((2 * ROWS, CELLS), jnp.float32)
    spread_scratch = pltpu.VMEM((2 * ROWS, CELLS), jnp.bfloat16)
    whole_scratch = pltpu.VMEM((chips, 2, OWN, CELLS), jnp.bfloat16)
    mine, slope_shape = shape((PAIR, CELLS)), shape((PAIR, CELLS), jnp.float32)

    act, *slopes = local_call(first_kernel, (mine, slope_shape, slope_shape), 2, [taps_scratch])(
        near, filters
    )
    after = lax.optimization_barrier
    outs, dpres = [act], []
    for step in range(ROUNDS):
        last = step + 1 == ROUNDS
        outs[step], near, filters = after((outs[step], near, filters))
        received = lax.ppermute(outs[step], ("section", "chip", "core"), hops[step])
        if step == 0:
            far = lax.ppermute(near, "core", [(0, 1), (1, 0)])
        elif step == 2:
            rest = local_call(slope_kernel, (slope_shape,) * 2, 3, [taps_scratch, whole_scratch], LIGHT)(
                filters, near, far
            )
            received, *rest = after((received, *rest))
            slopes.extend(rest)
        sent_shape = shape((2 * chips, OWN, CELLS) if last else (chips, PAIR, CELLS))
        sent, dpre = local_call(
            functools.partial(start_kernel, step),
            (sent_shape, mine),
            4,
            [spread_scratch],
        )(received, outside[step], slopes[step], filters)
        dpres.append(dpre)
        if last:
            break
        arrived = lax.all_to_all(sent, "chip", 0, 0)
        outs.append(local_call(finish_kernel, mine, 2, [taps_scratch])(arrived, filters))

    sent, *dpres = after((sent, *dpres))
    partials = lax.all_to_all(sent, ("chip", "core"), 0, 0)
    parcel = local_call(pack_kernel, shape((2 * ROUNDS - 1, OWN, CELLS)), 8, [], LIGHT)(
        *outs, *dpres
    )
    parcels = lax.all_gather(parcel, "core", axis=0)
    filter_grad, acts = local_call(
        filter_kernel,
        (shape((ROWS, CHANNELS), jnp.float32), shape((ROUNDS, OWN, CELLS))),
        11,
        [pltpu.VMEM((ROWS, CELLS), jnp.bfloat16), whole_scratch],
        LIGHT,
    )(near, far, parcels, *outs, *dpres)
    partials, filter_grad = lax.optimization_barrier((partials, filter_grad))
    grads = local_call(last_kernel, shape((ROUNDS, OWN, CELLS)), 5, [])(
        partials, parcels, *outs[1:]
    )
    filter_grad = jnp.transpose(filter_grad.reshape(TAPS, OWN, CHANNELS), (1, 0, 2))
    return acts[None], grads[None], filter_grad[None]


def solution(mesh):
    sections = mesh.shape["section"]
    fine = Mesh(mesh.devices.reshape(sections, -1, 2), ("section", "chip", "core"))
    chan = ("chip", "core")
    return jax.shard_map(
        lambda *arrays: body(sections, *arrays),
        mesh=fine,
        in_specs=(
            P(None, chan, None),
            P("section", chan, None),
            P("section", chan, None),
            P("section", None, chan, None),
            P("section", chan, None, None),
            P(None, chan, None),
        ),
        out_specs=(
            P("section", None, chan, None),
            P("section", None, chan, None),
            P("section", chan, None, None),
        ),
        check_vma=False,
    )
```

```python
import functools

import jax
import jax.numpy as jnp
from jax import lax
from jax.experimental import pallas as pl
from jax.experimental.pallas import tpu as pltpu
from jax.sharding import Mesh, PartitionSpec as P


SX, SY, SZ = 4, 8, 8
CELLS = SX * SY * SZ
TAPS = 27
OWN = 16
PAIR = 32
ROUNDS = 4
CHANNELS = 512
ROWS = TAPS * OWN
STEPS = (SY * SZ, SZ, 1)
EXTENT = (SX, SY, SZ)
VMEM_LIMIT = 16 * 1024 * 1024
LIGHT = pl.CostEstimate(flops=1, transcendentals=0, bytes_accessed=1)


def coordinates(rows):
    cell = lax.broadcasted_iota(jnp.int32, (rows, CELLS), 1)
    return (cell >> 6, (cell >> 3) & 7, cell & 7)


def moved(value, where, axis, step):
    if step == 0:
        return value
    rolled = pltpu.roll(value, (-step * STEPS[axis]) % CELLS, 1)
    place = where[axis]
    inside = place < EXTENT[axis] - 1 if step > 0 else place > 0
    return jnp.where(inside, rolled, 0.0)


def tap_total(taps, base, where):
    total = None
    for i in range(3):
        plane = None
        for j in range(3):
            line = None
            for l in range(3):
                start = base + OWN * (9 * i + 3 * j + l)
                term = moved(taps[start : start + OWN, :], where, 2, l - 1)
                line = term if line is None else line + term
            line = moved(line, where, 1, j - 1)
            plane = line if plane is None else plane + line
        plane = moved(plane, where, 0, i - 1)
        total = plane if total is None else total + plane
    return total


def spread_into(spread, base, value, where):
    for i in range(3):
        plane = moved(value, where, 0, 1 - i)
        for j in range(3):
            line = moved(plane, where, 1, 1 - j)
            for l in range(3):
                start = base + OWN * (9 * i + 3 * j + l)
                spread[start : start + OWN, :] = moved(line, where, 2, 1 - l).astype(jnp.bfloat16)


def slope_into(slope, filters, whole, taps, where):
    taps[...] = jnp.dot(filters[...], whole.reshape(CHANNELS, CELLS), preferred_element_type=jnp.float32)
    for c in range(2):
        pre = tap_total(taps, ROWS * c, where)
        logistic = 1.0 / (1.0 + jnp.exp(-pre))
        slope[OWN * c : OWN * (c + 1), :] = logistic * (1.0 + pre * (1.0 - logistic))


def silu_into(out, filters, whole, taps, where):
    taps[...] = jnp.dot(filters[...], whole.reshape(CHANNELS, CELLS), preferred_element_type=jnp.float32)
    for c in range(2):
        pre = tap_total(taps, ROWS * c, where)
        out[OWN * c : OWN * (c + 1), :] = (pre / (1.0 + jnp.exp(-pre))).astype(jnp.bfloat16)


def joined(even, odd, whole):
    whole[:, 0] = even[:, 4]
    whole[:, 1] = odd[:, 4]
    return whole[...]


def first_kernel(near, filters, act, first, second, taps):
    where = coordinates(OWN)

    @pl.when(lax.axis_index("core") == 0)
    def _():
        silu_into(act, filters, near[:, 0:2], taps, where)
        for slope in (first, second):
            slope[...] = jnp.zeros_like(slope)

    @pl.when(lax.axis_index("core") != 0)
    def _():
        act[...] = jnp.zeros_like(act)
        slope_into(first, filters, near[:, 0:2], taps, where)
        slope_into(second, filters, near[:, 2:4], taps, where)


def slope_kernel(filters, near, far, third, fourth, taps, whole):
    @pl.when(lax.axis_index("core") == 0)
    def _():
        for slope in (third, fourth):
            slope[...] = jnp.zeros_like(slope)

    @pl.when(lax.axis_index("core") != 0)
    def _():
        where = coordinates(OWN)
        slope_into(third, filters, far[:, 2:4], taps, where)
        slope_into(fourth, filters, joined(far, near, whole), taps, where)


def sum_into(out, arrived):
    total = arrived[0].astype(jnp.float32)
    for p in range(1, arrived.shape[0]):
        total = total + arrived[p].astype(jnp.float32)
    out[...] = total.astype(jnp.bfloat16)


def finish_kernel(arrived, filters, out, taps):
    @pl.when(lax.axis_index("core") == 0)
    def _():
        silu_into(out, filters, arrived[...], taps, coordinates(OWN))

    @pl.when(lax.axis_index("core") != 0)
    def _():
        sum_into(out, arrived)


def pack_kernel(*refs):
    outs, dpres, parcel = refs[:4], refs[4:8], refs[8]

    @pl.when(lax.axis_index("core") == 0)
    def _():
        for r, pair in enumerate(outs):
            parcel[r] = pair[OWN:, :]
        for r in range(ROUNDS - 1):
            parcel[ROUNDS + r] = jnp.zeros((OWN, CELLS), jnp.bfloat16)

    @pl.when(lax.axis_index("core") != 0)
    def _():
        for r, pair in enumerate((*dpres, *outs[1:])):
            parcel[r] = pair[:OWN, :]


def last_kernel(arrived, parcels, second, third, fourth, grads):
    for r, pair in enumerate((second, third, fourth)):
        odd = pair[OWN:, :].astype(jnp.float32)
        even = parcels[1, ROUNDS + r].astype(jnp.float32)
        grads[r] = jnp.where(lax.axis_index("core") == 0, even, odd).astype(jnp.bfloat16)
    total = arrived[1].astype(jnp.float32)
    for d in range(3, arrived.shape[0], 2):
        total = total + arrived[d].astype(jnp.float32)
    grads[ROUNDS - 1] = total.astype(jnp.bfloat16)


def start_kernel(step, received, outside, slope, filters, sent, dpre, spread):
    last = step + 1 == ROUNDS
    section = lax.axis_index("section")
    edge = section == lax.axis_size("section") - 1
    backward_edge = True if step == 0 else edge
    take = jnp.where(lax.axis_index("core") == 0, section == 0, backward_edge)
    value = jnp.where(take, outside[...].astype(jnp.float32), received[...].astype(jnp.float32))

    @pl.when(lax.axis_index("core") == 0)
    def _():
        copy = value.astype(jnp.bfloat16)
        dpre[...] = copy
        if last:
            sent[...] = jnp.zeros_like(sent)
        else:
            for p in range(sent.shape[0]):
                sent[p] = copy

    @pl.when(lax.axis_index("core") != 0)
    def _():
        where = coordinates(OWN)
        rounded = (value * slope[...]).astype(jnp.bfloat16)
        dpre[...] = rounded
        wide = rounded.astype(jnp.float32)
        for c in range(2):
            spread_into(spread, ROWS * c, wide[OWN * c : OWN * (c + 1), :], where)
        part = lax.dot_general(
            filters[...], spread[...], (((0,), (0,)), ((), ())), preferred_element_type=jnp.float32
        )
        sent[...] = part.astype(jnp.bfloat16).reshape(sent.shape)


def filter_kernel(near, far, back_far, parcels, *refs):
    acts_pair, dpres, (out, acts, spread, whole) = refs[:4], refs[4:8], refs[8:]

    def total(even, odd, act_of, dpre_of):
        where = coordinates(OWN)
        stored = (
            lambda: odd[:, 0:2],
            lambda: odd[:, 2:4],
            lambda: even[:, 2:4],
            lambda: joined(even, odd, whole),
        )
        for r in range(ROUNDS):
            acts[r] = act_of(r)
            spread_into(spread, 0, dpre_of(r).astype(jnp.float32), where)
            term = lax.dot_general(
                spread[...],
                stored[r]().reshape(CHANNELS, CELLS),
                (((1,), (1,)), ((), ())),
                preferred_element_type=jnp.float32,
            )
            if r == 0:
                out[...] = term
            else:
                out[...] += term

    @pl.when(lax.axis_index("core") == 0)
    def _():
        total(near, back_far, lambda r: acts_pair[r][:OWN, :], lambda r: parcels[1, r])

    @pl.when(lax.axis_index("core") != 0)
    def _():
        total(far, near, lambda r: parcels[0, r], lambda r: dpres[r][OWN:, :])


def local_call(kernel, outs, count, scratch, cost=None):
    specs = [pl.BlockSpec(memory_space=pltpu.VMEM)] * count
    result = jax.tree.map(lambda _: pl.BlockSpec(memory_space=pltpu.VMEM), outs)
    return pl.pallas_call(
        kernel,
        out_shape=outs,
        in_specs=specs,
        out_specs=result,
        scratch_shapes=scratch,
        compiler_params=pltpu.CompilerParams(vmem_limit_bytes=VMEM_LIMIT),
        cost_estimate=cost,
    )


def shape(dims, dtype=jnp.bfloat16):
    return jax.ShapeDtypeStruct(dims, dtype)


def body(sections, inputs, front, back, saved, weights, cotangent):
    chips = CHANNELS // PAIR
    section = lax.axis_index("section")
    core = lax.axis_index("core")
    forward = core == 0
    ahead, behind = [], []
    for s in range(sections - 1):
        for p in range(chips):
            here = (s * chips + p) * 2
            ahead.append((here, here + 2 * chips))
            behind.append((here + 1 + 2 * chips, here + 1))
    hops = [ahead, ahead + behind, ahead + behind, behind]

    known = lax.all_gather(
        jnp.concatenate([jnp.where(section == 0, inputs[:1], front), saved[0]]), "core", axis=1, tiled=True
    )
    block = jnp.where(
        forward,
        jnp.concatenate([known[0], known[3], known[4, :OWN]]),
        jnp.concatenate([known[1], known[2], known[4, OWN:]]),
    ).reshape(5, OWN, CELLS)
    near = lax.all_to_all(jnp.broadcast_to(block[None], (chips,) + block.shape), "chip", 0, 0)

    filters = lax.all_gather(
        jnp.transpose(weights[0], (1, 0, 2)).reshape(ROWS, CHANNELS), "core", axis=0, tiled=True
    )
    ends = jnp.concatenate(
        [inputs[1:], jnp.where(section == sections - 1, cotangent[:1], back), cotangent[1:]]
    )
    ends = lax.all_gather(ends, "core", axis=1, tiled=True)
    outside = jnp.where(forward, jnp.concatenate([ends[:3], ends[2:3]]), ends[3:])

    taps_scratch = pltpu.VMEM((2 * ROWS, CELLS), jnp.float32)
    spread_scratch = pltpu.VMEM((2 * ROWS, CELLS), jnp.bfloat16)
    whole_scratch = pltpu.VMEM((chips, 2, OWN, CELLS), jnp.bfloat16)
    mine, slope_shape = shape((PAIR, CELLS)), shape((PAIR, CELLS), jnp.float32)

    act, *slopes = local_call(first_kernel, (mine, slope_shape, slope_shape), 2, [taps_scratch])(
        near, filters
    )
    after = lax.optimization_barrier
    outs, dpres = [act], []
    for step in range(ROUNDS):
        last = step + 1 == ROUNDS
        outs[step], near, filters = after((outs[step], near, filters))
        received = lax.ppermute(outs[step], ("section", "chip", "core"), hops[step])
        if step == 0:
            far = lax.ppermute(near, "core", [(0, 1)])
        elif step == 2:
            rest = local_call(slope_kernel, (slope_shape,) * 2, 3, [taps_scratch, whole_scratch], LIGHT)(
                filters, near, far
            )
            received, *rest = after((received, *rest))
            slopes.extend(rest)
        sent_shape = shape((2 * chips, OWN, CELLS) if last else (chips, PAIR, CELLS))
        sent, dpre = local_call(
            functools.partial(start_kernel, step),
            (sent_shape, mine),
            4,
            [spread_scratch],
        )(received, outside[step], slopes[step], filters)
        dpres.append(dpre)
        if last:
            break
        arrived = lax.all_to_all(sent, "chip", 0, 0)
        outs.append(local_call(finish_kernel, mine, 2, [taps_scratch])(arrived, filters))

    sent, near, *dpres = after((sent, near, *dpres))
    back_far = lax.ppermute(near, "core", [(1, 0)])
    partials = lax.all_to_all(sent, ("chip", "core"), 0, 0)
    parcel = local_call(pack_kernel, shape((2 * ROUNDS - 1, OWN, CELLS)), 8, [], LIGHT)(
        *outs, *dpres
    )
    parcels = lax.all_gather(parcel, "core", axis=0)
    filter_grad, acts = local_call(
        filter_kernel,
        (shape((ROWS, CHANNELS), jnp.float32), shape((ROUNDS, OWN, CELLS))),
        12,
        [pltpu.VMEM((ROWS, CELLS), jnp.bfloat16), whole_scratch],
        LIGHT,
    )(near, far, back_far, parcels, *outs, *dpres)
    partials, filter_grad = lax.optimization_barrier((partials, filter_grad))
    grads = local_call(last_kernel, shape((ROUNDS, OWN, CELLS)), 5, [])(
        partials, parcels, *outs[1:]
    )
    filter_grad = jnp.transpose(filter_grad.reshape(TAPS, OWN, CHANNELS), (1, 0, 2))
    return acts[None], grads[None], filter_grad[None]


def solution(mesh):
    sections = mesh.shape["section"]
    fine = Mesh(mesh.devices.reshape(sections, -1, 2), ("section", "chip", "core"))
    chan = ("chip", "core")
    return jax.shard_map(
        lambda *arrays: body(sections, *arrays),
        mesh=fine,
        in_specs=(
            P(None, chan, None),
            P("section", chan, None),
            P("section", chan, None),
            P("section", None, chan, None),
            P("section", chan, None, None),
            P(None, chan, None),
        ),
        out_specs=(
            P("section", None, chan, None),
            P("section", None, chan, None),
            P("section", chan, None, None),
        ),
        check_vma=False,
    )
```

```python
import functools

import jax
import jax.numpy as jnp
from jax import lax
from jax.experimental import pallas as pl
from jax.experimental.pallas import tpu as pltpu
from jax.sharding import Mesh, PartitionSpec as P


SX, SY, SZ = 4, 8, 8
CELLS = SX * SY * SZ
TAPS = 27
OWN = 16
PAIR = 32
ROUNDS = 4
CHANNELS = 512
ROWS = TAPS * OWN
STEPS = (SY * SZ, SZ, 1)
EXTENT = (SX, SY, SZ)
VMEM_LIMIT = 16 * 1024 * 1024
LIGHT = pl.CostEstimate(flops=1, transcendentals=0, bytes_accessed=1)


def coordinates(rows):
    cell = lax.broadcasted_iota(jnp.int32, (rows, CELLS), 1)
    return (cell >> 6, (cell >> 3) & 7, cell & 7)


def moved(value, where, axis, step):
    if step == 0:
        return value
    rolled = pltpu.roll(value, (-step * STEPS[axis]) % CELLS, 1)
    place = where[axis]
    inside = place < EXTENT[axis] - 1 if step > 0 else place > 0
    return jnp.where(inside, rolled, 0.0)


def tap_total(taps, base, where):
    total = None
    for i in range(3):
        plane = None
        for j in range(3):
            line = None
            for l in range(3):
                start = base + OWN * (9 * i + 3 * j + l)
                term = moved(taps[start : start + OWN, :], where, 2, l - 1)
                line = term if line is None else line + term
            line = moved(line, where, 1, j - 1)
            plane = line if plane is None else plane + line
        plane = moved(plane, where, 0, i - 1)
        total = plane if total is None else total + plane
    return total


def spread_into(spread, base, value, where):
    for i in range(3):
        plane = moved(value, where, 0, 1 - i)
        for j in range(3):
            line = moved(plane, where, 1, 1 - j)
            for l in range(3):
                start = base + OWN * (9 * i + 3 * j + l)
                spread[start : start + OWN, :] = moved(line, where, 2, 1 - l).astype(jnp.bfloat16)


def slope_into(slope, filters, whole, taps, where):
    taps[...] = jnp.dot(filters[...], whole.reshape(CHANNELS, CELLS), preferred_element_type=jnp.float32)
    for c in range(2):
        pre = tap_total(taps, ROWS * c, where)
        logistic = 1.0 / (1.0 + jnp.exp(-pre))
        slope[OWN * c : OWN * (c + 1), :] = logistic * (1.0 + pre * (1.0 - logistic))


def silu_into(out, filters, whole, taps, where):
    taps[...] = jnp.dot(filters[...], whole.reshape(CHANNELS, CELLS), preferred_element_type=jnp.float32)
    for c in range(2):
        pre = tap_total(taps, ROWS * c, where)
        out[OWN * c : OWN * (c + 1), :] = (pre / (1.0 + jnp.exp(-pre))).astype(jnp.bfloat16)


def joined(even, odd, whole):
    whole[:, 0] = even[:, 4]
    whole[:, 1] = odd[:, 4]
    return whole[...]


def first_kernel(near, filters, act, first, second, taps):
    where = coordinates(OWN)

    @pl.when(lax.axis_index("core") == 0)
    def _():
        silu_into(act, filters, near[:, 0:2], taps, where)
        for slope in (first, second):
            slope[...] = jnp.zeros_like(slope)

    @pl.when(lax.axis_index("core") != 0)
    def _():
        act[...] = jnp.zeros_like(act)
        slope_into(first, filters, near[:, 0:2], taps, where)
        slope_into(second, filters, near[:, 2:4], taps, where)


def slope_kernel(filters, near, far, third, fourth, taps, whole):
    @pl.when(lax.axis_index("core") == 0)
    def _():
        for slope in (third, fourth):
            slope[...] = jnp.zeros_like(slope)

    @pl.when(lax.axis_index("core") != 0)
    def _():
        where = coordinates(OWN)
        slope_into(third, filters, far[:, 2:4], taps, where)
        slope_into(fourth, filters, joined(far, near, whole), taps, where)


def sum_into(out, arrived):
    total = arrived[0].astype(jnp.float32)
    for p in range(1, arrived.shape[0]):
        total = total + arrived[p].astype(jnp.float32)
    out[...] = total.astype(jnp.bfloat16)


def sum_into(out, arrived):
    total = arrived[0].astype(jnp.float32)
    for p in range(1, arrived.shape[0]):
        total = total + arrived[p].astype(jnp.float32)
    out[...] = total.astype(jnp.bfloat16)


def finish_kernel(arrived, filters, out, taps):
    @pl.when(lax.axis_index("core") == 0)
    def _():
        silu_into(out, filters, arrived[...], taps, coordinates(OWN))

    @pl.when(lax.axis_index("core") != 0)
    def _():
        sum_into(out, arrived)


def sum_kernel(arrived, out):
    @pl.when(lax.axis_index("core") == 0)
    def _():
        out[...] = jnp.zeros_like(out)

    @pl.when(lax.axis_index("core") != 0)
    def _():
        sum_into(out, arrived)


def pack_kernel(arrived, filters, *refs):
    (*outs, grad), dpres, (act, parcel, taps) = refs[:4], refs[4:8], refs[8:]

    @pl.when(lax.axis_index("core") == 0)
    def _():
        silu_into(act, filters, arrived[...], taps, coordinates(OWN))
        for r, pair in enumerate((*outs, act)):
            parcel[r] = pair[OWN:, :]
        for r in range(ROUNDS - 1):
            parcel[ROUNDS + r] = jnp.zeros((OWN, CELLS), jnp.bfloat16)

    @pl.when(lax.axis_index("core") != 0)
    def _():
        act[...] = jnp.zeros_like(act)
        for r, pair in enumerate((*dpres, *outs[1:], grad)):
            parcel[r] = pair[:OWN, :]


def last_kernel(arrived, parcels, second, third, fourth, grads):
    for r, pair in enumerate((second, third, fourth)):
        odd = pair[OWN:, :].astype(jnp.float32)
        even = parcels[1, ROUNDS + r].astype(jnp.float32)
        grads[r] = jnp.where(lax.axis_index("core") == 0, even, odd).astype(jnp.bfloat16)
    total = arrived[1].astype(jnp.float32)
    for d in range(3, arrived.shape[0], 2):
        total = total + arrived[d].astype(jnp.float32)
    grads[ROUNDS - 1] = total.astype(jnp.bfloat16)


def start_kernel(step, received, outside, slope, filters, sent, dpre, spread):
    last = step + 1 == ROUNDS
    section = lax.axis_index("section")
    edge = section == lax.axis_size("section") - 1
    backward_edge = True if step == 0 else edge
    take = jnp.where(lax.axis_index("core") == 0, section == 0, backward_edge)
    value = jnp.where(take, outside[...].astype(jnp.float32), received[...].astype(jnp.float32))

    @pl.when(lax.axis_index("core") == 0)
    def _():
        copy = value.astype(jnp.bfloat16)
        dpre[...] = copy
        if last:
            sent[...] = jnp.zeros_like(sent)
        else:
            for p in range(sent.shape[0]):
                sent[p] = copy

    @pl.when(lax.axis_index("core") != 0)
    def _():
        where = coordinates(OWN)
        rounded = (value * slope[...]).astype(jnp.bfloat16)
        dpre[...] = rounded
        wide = rounded.astype(jnp.float32)
        for c in range(2):
            spread_into(spread, ROWS * c, wide[OWN * c : OWN * (c + 1), :], where)
        part = lax.dot_general(
            filters[...], spread[...], (((0,), (0,)), ((), ())), preferred_element_type=jnp.float32
        )
        sent[...] = part.astype(jnp.bfloat16).reshape(sent.shape)


def filter_kernel(near, far, back_far, parcels, *refs):
    acts_pair, dpres, (out, acts, spread, whole) = refs[:4], refs[4:8], refs[8:]

    def total(even, odd, act_of, dpre_of):
        where = coordinates(OWN)
        stored = (
            lambda: odd[:, 0:2],
            lambda: odd[:, 2:4],
            lambda: even[:, 2:4],
            lambda: joined(even, odd, whole),
        )
        for r in range(ROUNDS):
            acts[r] = act_of(r)
            spread_into(spread, 0, dpre_of(r).astype(jnp.float32), where)
            term = lax.dot_general(
                spread[...],
                stored[r]().reshape(CHANNELS, CELLS),
                (((1,), (1,)), ((), ())),
                preferred_element_type=jnp.float32,
            )
            if r == 0:
                out[...] = term
            else:
                out[...] += term

    @pl.when(lax.axis_index("core") == 0)
    def _():
        total(near, back_far, lambda r: acts_pair[r][:OWN, :], lambda r: parcels[1, r])

    @pl.when(lax.axis_index("core") != 0)
    def _():
        total(far, near, lambda r: parcels[0, r], lambda r: dpres[r][OWN:, :])


def local_call(kernel, outs, count, scratch, cost=None):
    specs = [pl.BlockSpec(memory_space=pltpu.VMEM)] * count
    result = jax.tree.map(lambda _: pl.BlockSpec(memory_space=pltpu.VMEM), outs)
    return pl.pallas_call(
        kernel,
        out_shape=outs,
        in_specs=specs,
        out_specs=result,
        scratch_shapes=scratch,
        compiler_params=pltpu.CompilerParams(vmem_limit_bytes=VMEM_LIMIT),
        cost_estimate=cost,
    )


def shape(dims, dtype=jnp.bfloat16):
    return jax.ShapeDtypeStruct(dims, dtype)


def body(sections, inputs, front, back, saved, weights, cotangent):
    chips = CHANNELS // PAIR
    section = lax.axis_index("section")
    core = lax.axis_index("core")
    forward = core == 0
    ahead, behind = [], []
    for s in range(sections - 1):
        for p in range(chips):
            here = (s * chips + p) * 2
            ahead.append((here, here + 2 * chips))
            behind.append((here + 1 + 2 * chips, here + 1))
    hops = [ahead, ahead + behind, ahead + behind, behind]

    known = lax.all_gather(
        jnp.concatenate([jnp.where(section == 0, inputs[:1], front), saved[0]]), "core", axis=1, tiled=True
    )
    block = jnp.where(
        forward,
        jnp.concatenate([known[0], known[3], known[4, :OWN]]),
        jnp.concatenate([known[1], known[2], known[4, OWN:]]),
    ).reshape(5, OWN, CELLS)
    near = lax.all_to_all(jnp.broadcast_to(block[None], (chips,) + block.shape), "chip", 0, 0)

    filters = lax.all_gather(
        jnp.transpose(weights[0], (1, 0, 2)).reshape(ROWS, CHANNELS), "core", axis=0, tiled=True
    )
    ends = jnp.concatenate(
        [inputs[1:], jnp.where(section == sections - 1, cotangent[:1], back), cotangent[1:]]
    )
    ends = lax.all_gather(ends, "core", axis=1, tiled=True)
    outside = jnp.where(forward, jnp.concatenate([ends[:3], ends[2:3]]), ends[3:])

    taps_scratch = pltpu.VMEM((2 * ROWS, CELLS), jnp.float32)
    spread_scratch = pltpu.VMEM((2 * ROWS, CELLS), jnp.bfloat16)
    whole_scratch = pltpu.VMEM((chips, 2, OWN, CELLS), jnp.bfloat16)
    mine, slope_shape = shape((PAIR, CELLS)), shape((PAIR, CELLS), jnp.float32)

    act, *slopes = local_call(first_kernel, (mine, slope_shape, slope_shape), 2, [taps_scratch])(
        near, filters
    )
    after = lax.optimization_barrier
    outs, dpres = [act], []
    for step in range(ROUNDS):
        last = step + 1 == ROUNDS
        outs[step], near, filters = after((outs[step], near, filters))
        received = lax.ppermute(outs[step], ("section", "chip", "core"), hops[step])
        if step == 0:
            far = lax.ppermute(near, "core", [(0, 1)])
        elif step == 2:
            rest = local_call(slope_kernel, (slope_shape,) * 2, 3, [taps_scratch, whole_scratch], LIGHT)(
                filters, near, far
            )
            received, *rest = after((received, *rest))
            slopes.extend(rest)
        sent_shape = shape((2 * chips, OWN, CELLS) if last else (chips, PAIR, CELLS))
        sent, dpre = local_call(
            functools.partial(start_kernel, step),
            (sent_shape, mine),
            4,
            [spread_scratch],
        )(received, outside[step], slopes[step], filters)
        dpres.append(dpre)
        if last:
            break
        arrived = lax.all_to_all(sent, "chip", 0, 0)
        if step + 2 < ROUNDS:
            outs.append(local_call(finish_kernel, mine, 2, [taps_scratch])(arrived, filters))
        else:
            outs.append(local_call(sum_kernel, mine, 1, [])(arrived))

    sent, near, arrived, *dpres = after((sent, near, arrived, *dpres))
    back_far = lax.ppermute(near, "core", [(1, 0)])
    partials = lax.all_to_all(sent, ("chip", "core"), 0, 0)
    act, parcel = local_call(
        pack_kernel, (mine, shape((2 * ROUNDS - 1, OWN, CELLS))), 10, [taps_scratch], LIGHT
    )(arrived, filters, *outs, *dpres)
    parcels = lax.all_gather(parcel, "core", axis=0)
    filter_grad, acts = local_call(
        filter_kernel,
        (shape((ROWS, CHANNELS), jnp.float32), shape((ROUNDS, OWN, CELLS))),
        12,
        [pltpu.VMEM((ROWS, CELLS), jnp.bfloat16), whole_scratch],
        LIGHT,
    )(near, far, back_far, parcels, *outs[:3], act, *dpres)
    partials, filter_grad = lax.optimization_barrier((partials, filter_grad))
    grads = local_call(last_kernel, shape((ROUNDS, OWN, CELLS)), 5, [])(
        partials, parcels, *outs[1:]
    )
    filter_grad = jnp.transpose(filter_grad.reshape(TAPS, OWN, CHANNELS), (1, 0, 2))
    return acts[None], grads[None], filter_grad[None]


def solution(mesh):
    sections = mesh.shape["section"]
    fine = Mesh(mesh.devices.reshape(sections, -1, 2), ("section", "chip", "core"))
    chan = ("chip", "core")
    return jax.shard_map(
        lambda *arrays: body(sections, *arrays),
        mesh=fine,
        in_specs=(
            P(None, chan, None),
            P("section", chan, None),
            P("section", chan, None),
            P("section", None, chan, None),
            P("section", chan, None, None),
            P(None, chan, None),
        ),
        out_specs=(
            P("section", None, chan, None),
            P("section", None, chan, None),
            P("section", chan, None, None),
        ),
        check_vma=False,
    )
```

```python
import functools

import jax
import jax.numpy as jnp
from jax import lax
from jax.experimental import pallas as pl
from jax.experimental.pallas import tpu as pltpu
from jax.sharding import Mesh, PartitionSpec as P


SX, SY, SZ = 4, 8, 8
CELLS = SX * SY * SZ
TAPS = 27
OWN = 16
PAIR = 32
ROUNDS = 4
CHANNELS = 512
ROWS = TAPS * OWN
STEPS = (SY * SZ, SZ, 1)
EXTENT = (SX, SY, SZ)
VMEM_LIMIT = 16 * 1024 * 1024
LIGHT = pl.CostEstimate(flops=1, transcendentals=0, bytes_accessed=1)


def coordinates(rows):
    cell = lax.broadcasted_iota(jnp.int32, (rows, CELLS), 1)
    return (cell >> 6, (cell >> 3) & 7, cell & 7)


def moved(value, where, axis, step):
    if step == 0:
        return value
    rolled = pltpu.roll(value, (-step * STEPS[axis]) % CELLS, 1)
    place = where[axis]
    inside = place < EXTENT[axis] - 1 if step > 0 else place > 0
    return jnp.where(inside, rolled, 0.0)


def tap_total(taps, base, where):
    total = None
    for i in range(3):
        plane = None
        for j in range(3):
            line = None
            for l in range(3):
                start = base + OWN * (9 * i + 3 * j + l)
                term = moved(taps[start : start + OWN, :], where, 2, l - 1)
                line = term if line is None else line + term
            line = moved(line, where, 1, j - 1)
            plane = line if plane is None else plane + line
        plane = moved(plane, where, 0, i - 1)
        total = plane if total is None else total + plane
    return total


def spread_into(spread, base, value, where):
    for i in range(3):
        plane = moved(value, where, 0, 1 - i)
        for j in range(3):
            line = moved(plane, where, 1, 1 - j)
            for l in range(3):
                start = base + OWN * (9 * i + 3 * j + l)
                spread[start : start + OWN, :] = moved(line, where, 2, 1 - l).astype(jnp.bfloat16)


def slope_into(slope, filters, whole, taps, where):
    taps[...] = jnp.dot(filters[...], whole.reshape(CHANNELS, CELLS), preferred_element_type=jnp.float32)
    for c in range(2):
        pre = tap_total(taps, ROWS * c, where)
        logistic = 1.0 / (1.0 + jnp.exp(-pre))
        slope[OWN * c : OWN * (c + 1), :] = logistic * (1.0 + pre * (1.0 - logistic))


def silu_into(out, filters, whole, taps, where):
    taps[...] = jnp.dot(filters[...], whole.reshape(CHANNELS, CELLS), preferred_element_type=jnp.float32)
    for c in range(2):
        pre = tap_total(taps, ROWS * c, where)
        out[OWN * c : OWN * (c + 1), :] = (pre / (1.0 + jnp.exp(-pre))).astype(jnp.bfloat16)


def joined(even, odd, whole):
    whole[:, 0] = even[:, 4]
    whole[:, 1] = odd[:, 4]
    return whole[...]


def first_kernel(near, filters, act, first, second, taps):
    where = coordinates(OWN)

    @pl.when(lax.axis_index("core") == 0)
    def _():
        silu_into(act, filters, near[:, 0:2], taps, where)

    @pl.when(lax.axis_index("core") != 0)
    def _():
        act[...] = jnp.zeros_like(act)
        slope_into(first, filters, near[:, 0:2], taps, where)
        slope_into(second, filters, near[:, 2:4], taps, where)


def slope_kernel(filters, near, far, third, fourth, taps, whole):
    @pl.when(lax.axis_index("core") != 0)
    def _():
        where = coordinates(OWN)
        slope_into(third, filters, far[:, 2:4], taps, where)
        slope_into(fourth, filters, joined(far, near, whole), taps, where)


def sum_into(out, arrived):
    total = arrived[0].astype(jnp.float32)
    for p in range(1, arrived.shape[0]):
        total = total + arrived[p].astype(jnp.float32)
    out[...] = total.astype(jnp.bfloat16)


def sum_into(out, arrived):
    total = arrived[0].astype(jnp.float32)
    for p in range(1, arrived.shape[0]):
        total = total + arrived[p].astype(jnp.float32)
    out[...] = total.astype(jnp.bfloat16)


def finish_kernel(arrived, filters, out, taps):
    @pl.when(lax.axis_index("core") == 0)
    def _():
        silu_into(out, filters, arrived[...], taps, coordinates(OWN))

    @pl.when(lax.axis_index("core") != 0)
    def _():
        sum_into(out, arrived)


def sum_kernel(arrived, out):
    @pl.when(lax.axis_index("core") != 0)
    def _():
        sum_into(out, arrived)


def pack_kernel(arrived, filters, *refs):
    (*outs, grad), dpres, (act, parcel, taps) = refs[:4], refs[4:8], refs[8:]

    @pl.when(lax.axis_index("core") == 0)
    def _():
        silu_into(act, filters, arrived[...], taps, coordinates(OWN))
        for r, pair in enumerate((*outs, act)):
            parcel[r] = pair[OWN:, :]
        for r in range(ROUNDS - 1):
            parcel[ROUNDS + r] = jnp.zeros((OWN, CELLS), jnp.bfloat16)

    @pl.when(lax.axis_index("core") != 0)
    def _():
        act[...] = jnp.zeros_like(act)
        for r, pair in enumerate((*dpres, *outs[1:], grad)):
            parcel[r] = pair[:OWN, :]


def last_kernel(arrived, parcels, second, third, fourth, grads):
    for r, pair in enumerate((second, third, fourth)):
        odd = pair[OWN:, :].astype(jnp.float32)
        even = parcels[1, ROUNDS + r].astype(jnp.float32)
        grads[r] = jnp.where(lax.axis_index("core") == 0, even, odd).astype(jnp.bfloat16)
    total = arrived[1].astype(jnp.float32)
    for d in range(3, arrived.shape[0], 2):
        total = total + arrived[d].astype(jnp.float32)
    grads[ROUNDS - 1] = total.astype(jnp.bfloat16)


def start_kernel(step, received, outside, slope, filters, sent, dpre, spread):
    last = step + 1 == ROUNDS
    section = lax.axis_index("section")
    edge = section == lax.axis_size("section") - 1
    backward_edge = True if step == 0 else edge
    take = jnp.where(lax.axis_index("core") == 0, section == 0, backward_edge)
    value = jnp.where(take, outside[...].astype(jnp.float32), received[...].astype(jnp.float32))

    @pl.when(lax.axis_index("core") == 0)
    def _():
        copy = value.astype(jnp.bfloat16)
        dpre[...] = copy
        if not last:
            for p in range(sent.shape[0]):
                sent[p] = copy

    @pl.when(lax.axis_index("core") != 0)
    def _():
        where = coordinates(OWN)
        rounded = (value * slope[...]).astype(jnp.bfloat16)
        dpre[...] = rounded
        wide = rounded.astype(jnp.float32)
        for c in range(2):
            spread_into(spread, ROWS * c, wide[OWN * c : OWN * (c + 1), :], where)
        part = lax.dot_general(
            filters[...], spread[...], (((0,), (0,)), ((), ())), preferred_element_type=jnp.float32
        )
        sent[...] = part.astype(jnp.bfloat16).reshape(sent.shape)


def filter_kernel(near, far, back_far, parcels, *refs):
    acts_pair, dpres, (out, acts, spread, whole) = refs[:4], refs[4:8], refs[8:]

    def total(even, odd, act_of, dpre_of):
        where = coordinates(OWN)
        stored = (
            lambda: odd[:, 0:2],
            lambda: odd[:, 2:4],
            lambda: even[:, 2:4],
            lambda: joined(even, odd, whole),
        )
        for r in range(ROUNDS):
            acts[r] = act_of(r)
            spread_into(spread, 0, dpre_of(r).astype(jnp.float32), where)
            term = lax.dot_general(
                spread[...],
                stored[r]().reshape(CHANNELS, CELLS),
                (((1,), (1,)), ((), ())),
                preferred_element_type=jnp.float32,
            )
            if r == 0:
                out[...] = term
            else:
                out[...] += term

    @pl.when(lax.axis_index("core") == 0)
    def _():
        total(near, back_far, lambda r: acts_pair[r][:OWN, :], lambda r: parcels[1, r])

    @pl.when(lax.axis_index("core") != 0)
    def _():
        total(far, near, lambda r: parcels[0, r], lambda r: dpres[r][OWN:, :])


def local_call(kernel, outs, count, scratch, cost=None):
    specs = [pl.BlockSpec(memory_space=pltpu.VMEM)] * count
    result = jax.tree.map(lambda _: pl.BlockSpec(memory_space=pltpu.VMEM), outs)
    return pl.pallas_call(
        kernel,
        out_shape=outs,
        in_specs=specs,
        out_specs=result,
        scratch_shapes=scratch,
        compiler_params=pltpu.CompilerParams(vmem_limit_bytes=VMEM_LIMIT),
        cost_estimate=cost,
    )


def shape(dims, dtype=jnp.bfloat16):
    return jax.ShapeDtypeStruct(dims, dtype)


def body(sections, inputs, front, back, saved, weights, cotangent):
    chips = CHANNELS // PAIR
    section = lax.axis_index("section")
    core = lax.axis_index("core")
    forward = core == 0
    ahead, behind = [], []
    for s in range(sections - 1):
        for p in range(chips):
            here = (s * chips + p) * 2
            ahead.append((here, here + 2 * chips))
            behind.append((here + 1 + 2 * chips, here + 1))
    hops = [ahead, ahead + behind, ahead + behind, behind]

    known = lax.all_gather(
        jnp.concatenate([jnp.where(section == 0, inputs[:1], front), saved[0]]), "core", axis=1, tiled=True
    )
    block = jnp.where(
        forward,
        jnp.concatenate([known[0], known[3], known[4, :OWN]]),
        jnp.concatenate([known[1], known[2], known[4, OWN:]]),
    ).reshape(5, OWN, CELLS)
    near = lax.all_to_all(jnp.broadcast_to(block[None], (chips,) + block.shape), "chip", 0, 0)

    filters = lax.all_gather(
        jnp.transpose(weights[0], (1, 0, 2)).reshape(ROWS, CHANNELS), "core", axis=0, tiled=True
    )
    ends = jnp.concatenate(
        [inputs[1:], jnp.where(section == sections - 1, cotangent[:1], back), cotangent[1:]]
    )
    ends = lax.all_gather(ends, "core", axis=1, tiled=True)
    outside = jnp.where(forward, jnp.concatenate([ends[:3], ends[2:3]]), ends[3:])

    taps_scratch = pltpu.VMEM((2 * ROWS, CELLS), jnp.float32)
    spread_scratch = pltpu.VMEM((2 * ROWS, CELLS), jnp.bfloat16)
    whole_scratch = pltpu.VMEM((chips, 2, OWN, CELLS), jnp.bfloat16)
    mine, slope_shape = shape((PAIR, CELLS)), shape((PAIR, CELLS), jnp.float32)

    act, *slopes = local_call(first_kernel, (mine, slope_shape, slope_shape), 2, [taps_scratch])(
        near, filters
    )
    after = lax.optimization_barrier
    outs, dpres = [act], []
    for step in range(ROUNDS):
        last = step + 1 == ROUNDS
        outs[step], near, filters = after((outs[step], near, filters))
        received = lax.ppermute(outs[step], ("section", "chip", "core"), hops[step])
        if step == 0:
            far = lax.ppermute(near, "core", [(0, 1)])
        elif step == 2:
            rest = local_call(slope_kernel, (slope_shape,) * 2, 3, [taps_scratch, whole_scratch], LIGHT)(
                filters, near, far
            )
            received, *rest = after((received, *rest))
            slopes.extend(rest)
        sent_shape = shape((2 * chips, OWN, CELLS) if last else (chips, PAIR, CELLS))
        sent, dpre = local_call(
            functools.partial(start_kernel, step),
            (sent_shape, mine),
            4,
            [spread_scratch],
        )(received, outside[step], slopes[step], filters)
        dpres.append(dpre)
        if last:
            break
        arrived = lax.all_to_all(sent, "chip", 0, 0)
        if step + 2 < ROUNDS:
            outs.append(local_call(finish_kernel, mine, 2, [taps_scratch])(arrived, filters))
        else:
            outs.append(local_call(sum_kernel, mine, 1, [])(arrived))

    sent, near, arrived, *dpres = after((sent, near, arrived, *dpres))
    back_far = lax.ppermute(near, "core", [(1, 0)])
    partials = lax.all_to_all(sent, ("chip", "core"), 0, 0)
    act, parcel = local_call(
        pack_kernel, (mine, shape((2 * ROUNDS - 1, OWN, CELLS))), 10, [taps_scratch], LIGHT
    )(arrived, filters, *outs, *dpres)
    parcels = lax.all_gather(parcel, "core", axis=0)
    filter_grad, acts = local_call(
        filter_kernel,
        (shape((ROWS, CHANNELS), jnp.float32), shape((ROUNDS, OWN, CELLS))),
        12,
        [pltpu.VMEM((ROWS, CELLS), jnp.bfloat16), whole_scratch],
        LIGHT,
    )(near, far, back_far, parcels, *outs[:3], act, *dpres)
    partials, filter_grad = lax.optimization_barrier((partials, filter_grad))
    grads = local_call(last_kernel, shape((ROUNDS, OWN, CELLS)), 5, [])(
        partials, parcels, *outs[1:]
    )
    filter_grad = jnp.transpose(filter_grad.reshape(TAPS, OWN, CHANNELS), (1, 0, 2))
    return acts[None], grads[None], filter_grad[None]


def solution(mesh):
    sections = mesh.shape["section"]
    fine = Mesh(mesh.devices.reshape(sections, -1, 2), ("section", "chip", "core"))
    chan = ("chip", "core")
    return jax.shard_map(
        lambda *arrays: body(sections, *arrays),
        mesh=fine,
        in_specs=(
            P(None, chan, None),
            P("section", chan, None),
            P("section", chan, None),
            P("section", None, chan, None),
            P("section", chan, None, None),
            P(None, chan, None),
        ),
        out_specs=(
            P("section", None, chan, None),
            P("section", None, chan, None),
            P("section", chan, None, None),
        ),
        check_vma=False,
    )
```

```python
import functools

import jax
import jax.numpy as jnp
from jax import lax
from jax.experimental import pallas as pl
from jax.experimental.pallas import tpu as pltpu
from jax.sharding import Mesh, PartitionSpec as P


SX, SY, SZ = 4, 8, 8
CELLS = SX * SY * SZ
TAPS = 27
OWN = 16
PAIR = 32
ROUNDS = 4
CHANNELS = 512
ROWS = TAPS * OWN
STEPS = (SY * SZ, SZ, 1)
EXTENT = (SX, SY, SZ)
VMEM_LIMIT = 16 * 1024 * 1024
LIGHT = pl.CostEstimate(flops=1, transcendentals=0, bytes_accessed=1)


def coordinates(rows):
    cell = lax.broadcasted_iota(jnp.int32, (rows, CELLS), 1)
    return (cell >> 6, (cell >> 3) & 7, cell & 7)


def moved(value, where, axis, step):
    if step == 0:
        return value
    rolled = pltpu.roll(value, (-step * STEPS[axis]) % CELLS, 1)
    place = where[axis]
    inside = place < EXTENT[axis] - 1 if step > 0 else place > 0
    return jnp.where(inside, rolled, 0.0)


def tap_total(taps, base, where):
    total = None
    for i in range(3):
        plane = None
        for j in range(3):
            line = None
            for l in range(3):
                start = base + OWN * (9 * i + 3 * j + l)
                term = moved(taps[start : start + OWN, :], where, 2, l - 1)
                line = term if line is None else line + term
            line = moved(line, where, 1, j - 1)
            plane = line if plane is None else plane + line
        plane = moved(plane, where, 0, i - 1)
        total = plane if total is None else total + plane
    return total


def spread_into(spread, base, value, where):
    for i in range(3):
        plane = moved(value, where, 0, 1 - i)
        for j in range(3):
            line = moved(plane, where, 1, 1 - j)
            for l in range(3):
                start = base + OWN * (9 * i + 3 * j + l)
                spread[start : start + OWN, :] = moved(line, where, 2, 1 - l).astype(jnp.bfloat16)


def slope_into(slope, filters, whole, taps, where):
    taps[...] = jnp.dot(filters[...], whole.reshape(CHANNELS, CELLS), preferred_element_type=jnp.float32)
    for c in range(2):
        pre = tap_total(taps, ROWS * c, where)
        logistic = 1.0 / (1.0 + jnp.exp(-pre))
        slope[OWN * c : OWN * (c + 1), :] = logistic * (1.0 + pre * (1.0 - logistic))


def silu_into(out, filters, whole, taps, where):
    taps[...] = jnp.dot(filters[...], whole.reshape(CHANNELS, CELLS), preferred_element_type=jnp.float32)
    for c in range(2):
        pre = tap_total(taps, ROWS * c, where)
        out[OWN * c : OWN * (c + 1), :] = (pre / (1.0 + jnp.exp(-pre))).astype(jnp.bfloat16)


def joined(even, odd, whole):
    whole[:, 0] = even[:, 4]
    whole[:, 1] = odd[:, 4]
    return whole[...]


def first_kernel(near, filters, act, first, second, taps):
    where = coordinates(OWN)

    @pl.when(lax.axis_index("core") == 0)
    def _():
        silu_into(act, filters, near[:, 0:2], taps, where)

    @pl.when(lax.axis_index("core") != 0)
    def _():
        slope_into(first, filters, near[:, 0:2], taps, where)
        slope_into(second, filters, near[:, 2:4], taps, where)


def slope_kernel(filters, near, far, third, fourth, taps, whole):
    @pl.when(lax.axis_index("core") != 0)
    def _():
        where = coordinates(OWN)
        slope_into(third, filters, far[:, 2:4], taps, where)
        slope_into(fourth, filters, joined(far, near, whole), taps, where)


def sum_into(out, arrived):
    total = arrived[0].astype(jnp.float32)
    for p in range(1, arrived.shape[0]):
        total = total + arrived[p].astype(jnp.float32)
    out[...] = total.astype(jnp.bfloat16)


def sum_into(out, arrived):
    total = arrived[0].astype(jnp.float32)
    for p in range(1, arrived.shape[0]):
        total = total + arrived[p].astype(jnp.float32)
    out[...] = total.astype(jnp.bfloat16)


def finish_kernel(arrived, filters, out, taps):
    @pl.when(lax.axis_index("core") == 0)
    def _():
        silu_into(out, filters, arrived[...], taps, coordinates(OWN))

    @pl.when(lax.axis_index("core") != 0)
    def _():
        sum_into(out, arrived)


def sum_kernel(arrived, out):
    @pl.when(lax.axis_index("core") != 0)
    def _():
        sum_into(out, arrived)


def pack_kernel(arrived, filters, *refs):
    (*outs, grad), dpres, (act, parcel, taps) = refs[:4], refs[4:8], refs[8:]

    @pl.when(lax.axis_index("core") == 0)
    def _():
        silu_into(act, filters, arrived[...], taps, coordinates(OWN))
        for r, pair in enumerate((*outs, act)):
            parcel[r] = pair[OWN:, :]
        for r in range(ROUNDS - 1):
            parcel[ROUNDS + r] = jnp.zeros((OWN, CELLS), jnp.bfloat16)

    @pl.when(lax.axis_index("core") != 0)
    def _():
        for r, pair in enumerate((*dpres, *outs[1:], grad)):
            parcel[r] = pair[:OWN, :]


def last_kernel(arrived, parcels, second, third, fourth, grads):
    for r, pair in enumerate((second, third, fourth)):
        odd = pair[OWN:, :].astype(jnp.float32)
        even = parcels[1, ROUNDS + r].astype(jnp.float32)
        grads[r] = jnp.where(lax.axis_index("core") == 0, even, odd).astype(jnp.bfloat16)
    total = arrived[1].astype(jnp.float32)
    for d in range(3, arrived.shape[0], 2):
        total = total + arrived[d].astype(jnp.float32)
    grads[ROUNDS - 1] = total.astype(jnp.bfloat16)


def start_kernel(step, received, outside, slope, filters, sent, dpre, spread):
    last = step + 1 == ROUNDS
    section = lax.axis_index("section")
    edge = section == lax.axis_size("section") - 1
    backward_edge = True if step == 0 else edge
    take = jnp.where(lax.axis_index("core") == 0, section == 0, backward_edge)
    value = jnp.where(take, outside[...].astype(jnp.float32), received[...].astype(jnp.float32))

    @pl.when(lax.axis_index("core") == 0)
    def _():
        copy = value.astype(jnp.bfloat16)
        if not last:
            for p in range(sent.shape[0]):
                sent[p] = copy

    @pl.when(lax.axis_index("core") != 0)
    def _():
        where = coordinates(OWN)
        rounded = (value * slope[...]).astype(jnp.bfloat16)
        dpre[...] = rounded
        wide = rounded.astype(jnp.float32)
        for c in range(2):
            spread_into(spread, ROWS * c, wide[OWN * c : OWN * (c + 1), :], where)
        part = lax.dot_general(
            filters[...], spread[...], (((0,), (0,)), ((), ())), preferred_element_type=jnp.float32
        )
        sent[...] = part.astype(jnp.bfloat16).reshape(sent.shape)


def filter_kernel(near, far, back_far, parcels, *refs):
    acts_pair, dpres, (out, acts, spread, whole) = refs[:4], refs[4:8], refs[8:]

    def total(even, odd, act_of, dpre_of):
        where = coordinates(OWN)
        stored = (
            lambda: odd[:, 0:2],
            lambda: odd[:, 2:4],
            lambda: even[:, 2:4],
            lambda: joined(even, odd, whole),
        )
        for r in range(ROUNDS):
            acts[r] = act_of(r)
            spread_into(spread, 0, dpre_of(r).astype(jnp.float32), where)
            term = lax.dot_general(
                spread[...],
                stored[r]().reshape(CHANNELS, CELLS),
                (((1,), (1,)), ((), ())),
                preferred_element_type=jnp.float32,
            )
            if r == 0:
                out[...] = term
            else:
                out[...] += term

    @pl.when(lax.axis_index("core") == 0)
    def _():
        total(near, back_far, lambda r: acts_pair[r][:OWN, :], lambda r: parcels[1, r])

    @pl.when(lax.axis_index("core") != 0)
    def _():
        total(far, near, lambda r: parcels[0, r], lambda r: dpres[r][OWN:, :])


def local_call(kernel, outs, count, scratch, cost=None):
    specs = [pl.BlockSpec(memory_space=pltpu.VMEM)] * count
    result = jax.tree.map(lambda _: pl.BlockSpec(memory_space=pltpu.VMEM), outs)
    return pl.pallas_call(
        kernel,
        out_shape=outs,
        in_specs=specs,
        out_specs=result,
        scratch_shapes=scratch,
        compiler_params=pltpu.CompilerParams(vmem_limit_bytes=VMEM_LIMIT),
        cost_estimate=cost,
    )


def shape(dims, dtype=jnp.bfloat16):
    return jax.ShapeDtypeStruct(dims, dtype)


def body(sections, inputs, front, back, saved, weights, cotangent):
    chips = CHANNELS // PAIR
    section = lax.axis_index("section")
    core = lax.axis_index("core")
    forward = core == 0
    ahead, behind = [], []
    for s in range(sections - 1):
        for p in range(chips):
            here = (s * chips + p) * 2
            ahead.append((here, here + 2 * chips))
            behind.append((here + 1 + 2 * chips, here + 1))
    hops = [ahead, ahead + behind, ahead + behind, behind]

    known = lax.all_gather(
        jnp.concatenate([jnp.where(section == 0, inputs[:1], front), saved[0]]), "core", axis=1, tiled=True
    )
    block = jnp.where(
        forward,
        jnp.concatenate([known[0], known[3], known[4, :OWN]]),
        jnp.concatenate([known[1], known[2], known[4, OWN:]]),
    ).reshape(5, OWN, CELLS)
    near = lax.all_to_all(jnp.broadcast_to(block[None], (chips,) + block.shape), "chip", 0, 0)

    filters = lax.all_gather(
        jnp.transpose(weights[0], (1, 0, 2)).reshape(ROWS, CHANNELS), "core", axis=0, tiled=True
    )
    ends = jnp.concatenate(
        [inputs[1:], jnp.where(section == sections - 1, cotangent[:1], back), cotangent[1:]]
    )
    ends = lax.all_gather(ends, "core", axis=1, tiled=True)
    outside = jnp.where(forward, jnp.concatenate([ends[:3], ends[2:3]]), ends[3:])

    taps_scratch = pltpu.VMEM((2 * ROWS, CELLS), jnp.float32)
    spread_scratch = pltpu.VMEM((2 * ROWS, CELLS), jnp.bfloat16)
    whole_scratch = pltpu.VMEM((chips, 2, OWN, CELLS), jnp.bfloat16)
    mine, slope_shape = shape((PAIR, CELLS)), shape((PAIR, CELLS), jnp.float32)

    act, *slopes = local_call(first_kernel, (mine, slope_shape, slope_shape), 2, [taps_scratch])(
        near, filters
    )
    after = lax.optimization_barrier
    outs, dpres = [act], []
    for step in range(ROUNDS):
        last = step + 1 == ROUNDS
        outs[step], near, filters = after((outs[step], near, filters))
        received = lax.ppermute(outs[step], ("section", "chip", "core"), hops[step])
        if step == 0:
            far = lax.ppermute(near, "core", [(0, 1)])
        elif step == 2:
            rest = local_call(slope_kernel, (slope_shape,) * 2, 3, [taps_scratch, whole_scratch], LIGHT)(
                filters, near, far
            )
            received, *rest = after((received, *rest))
            slopes.extend(rest)
        sent_shape = shape((2 * chips, OWN, CELLS) if last else (chips, PAIR, CELLS))
        sent, dpre = local_call(
            functools.partial(start_kernel, step),
            (sent_shape, mine),
            4,
            [spread_scratch],
        )(received, outside[step], slopes[step], filters)
        dpres.append(dpre)
        if last:
            break
        arrived = lax.all_to_all(sent, "chip", 0, 0)
        if step + 2 < ROUNDS:
            outs.append(local_call(finish_kernel, mine, 2, [taps_scratch])(arrived, filters))
        else:
            outs.append(local_call(sum_kernel, mine, 1, [])(arrived))

    sent, near, arrived, *dpres = after((sent, near, arrived, *dpres))
    back_far = lax.ppermute(near, "core", [(1, 0)])
    partials = lax.all_to_all(sent, ("chip", "core"), 0, 0)
    act, parcel = local_call(
        pack_kernel, (mine, shape((2 * ROUNDS - 1, OWN, CELLS))), 10, [taps_scratch], LIGHT
    )(arrived, filters, *outs, *dpres)
    parcels = lax.all_gather(parcel, "core", axis=0)
    filter_grad, acts = local_call(
        filter_kernel,
        (shape((ROWS, CHANNELS), jnp.float32), shape((ROUNDS, OWN, CELLS))),
        12,
        [pltpu.VMEM((ROWS, CELLS), jnp.bfloat16), whole_scratch],
        LIGHT,
    )(near, far, back_far, parcels, *outs[:3], act, *dpres)
    partials, filter_grad = lax.optimization_barrier((partials, filter_grad))
    grads = local_call(last_kernel, shape((ROUNDS, OWN, CELLS)), 5, [])(
        partials, parcels, *outs[1:]
    )
    filter_grad = jnp.transpose(filter_grad.reshape(TAPS, OWN, CHANNELS), (1, 0, 2))
    return acts[None], grads[None], filter_grad[None]


def solution(mesh):
    sections = mesh.shape["section"]
    fine = Mesh(mesh.devices.reshape(sections, -1, 2), ("section", "chip", "core"))
    chan = ("chip", "core")
    return jax.shard_map(
        lambda *arrays: body(sections, *arrays),
        mesh=fine,
        in_specs=(
            P(None, chan, None),
            P("section", chan, None),
            P("section", chan, None),
            P("section", None, chan, None),
            P("section", chan, None, None),
            P(None, chan, None),
        ),
        out_specs=(
            P("section", None, chan, None),
            P("section", None, chan, None),
            P("section", chan, None, None),
        ),
        check_vma=False,
    )
```
